32 devices in a mesh: videos: 2 (over y), rows: 4 (over z), cols: 4 (over x, core).
Axes of the slice: x: 2, y: 2, z: 4, core: 2. Of those that a mesh axis runs over, the one named last changes fastest.
Arguments:
- hidden: bfloat16 [2, 16, 128, 384], P('videos', 'rows', 'cols'), parts along dimension 0, may hold values from -40 to 40
- frame_cache: bfloat16 [2, 2, 16, 128, 384], P('videos', None, 'rows', 'cols'), parts along dimension 0, may hold values from -6 to 6
- shortcut: bfloat16 [2, 16, 128, 384], P('videos', 'rows', 'cols'), parts along dimension 0, may hold values from -40 to 40
- gain_one: float32 [384], replicated, may hold values from 0.5 to 1.5
- conv_weight: bfloat16 [3, 3, 3, 384, 384], replicated, may hold values from -0.0625 to 0.0625
- conv_bias: float32 [384], replicated, may hold values from -2 to 2
- gain_two: float32 [384], replicated, may hold values from 0.5 to 1.5
- query_weight: bfloat16 [384, 384], replicated, may hold values from -1 to 1
- query_bias: float32 [384], replicated, may hold values from -3 to 3
- key_weight: bfloat16 [384, 384], replicated, may hold values from -1 to 1
- value_weight: bfloat16 [384, 384], replicated, may hold values from -0.3125 to 0.3125
- value_bias: float32 [384], replicated, may hold values from -3 to 3
- out_weight: bfloat16 [384, 384], replicated, may hold values from -0.3125 to 0.3125
- out_bias: float32 [384], replicated, may hold values from -2 to 2
Outputs:
- decoded: bfloat16 [2, 16, 128, 384], P('videos', 'rows', 'cols'), parts along dimension 0
The draws below stay inside these ranges and needn't reach their ends.
There are 2 independent parts, one for each index of `videos`. The reference program is written for one: setup_inputs(seed, part) draws one part's arguments, and reference() takes and returns one part's arrays. A program takes and returns all parts, laid end to end along the dimension named above; an argument that names none is the same for every part. Nothing has to cross between parts.
All inputs are finite; a program needn't handle non-finite values.
Results may differ from the reference program's by a relative error of at most 0.0065.
Values may be sent and summed in bfloat16 or wider, within the bound.
No kernel may reach another device: no remote copies, remote signals or barrier semaphores. Data moves between devices by JAX's collectives and lax.ppermute only.
A program may use at most 128 MiB of HBM per device.

```python
import math
import jax
import jax.numpy as jnp
from jax import lax

C = 384
H = 16
W = 128


def rough_field(key):
    standard = jax.random.truncated_normal(jax.random.fold_in(key, 1), -6.0, 6.0, (1, H, W, C), jnp.float32)
    row_place = jnp.arange(H, dtype=jnp.float32) / (H - 1)
    col_place = jnp.arange(W, dtype=jnp.float32) / (W - 1)
    spread_map = (3.0 ** (row_place - 0.5))[:, None] * (3.0 ** (col_place - 0.5))[None, :]
    return (standard * spread_map[None, :, :, None]).astype(jnp.bfloat16)


def draw_hidden(key, part):
    return rough_field(jax.random.fold_in(key, 101))


def draw_shortcut(key, part):
    return rough_field(jax.random.fold_in(key, 202))


def paired_weight(key, salt):
    own_part = jax.random.truncated_normal(jax.random.fold_in(key, salt), -5.0, 5.0, (C, C), jnp.float32)
    matrix = 1.4 * own_part / math.sqrt(C)
    return jnp.clip(matrix, -1.0, 1.0).astype(jnp.bfloat16)


def draw_query_weight(key, part):
    return paired_weight(key, 401)


def draw_key_weight(key, part):
    return paired_weight(key, 402)


def block_scale(stream_key, dims, cuts, least, largest):
    def one(dim, parts):
        heights = jax.random.uniform(jax.random.fold_in(jax.random.fold_in(stream_key, 6), dim), (parts,), jnp.float32, least / len(cuts), largest / len(cuts))
        return jnp.repeat(jnp.exp(heights), dims[dim] // parts).reshape((-1,) + (1,) * (len(dims) - dim - 1))

    factor_of = one(*cuts[0])
    for cut in cuts[1:]:
        factor_of = factor_of * one(*cut)
    return factor_of


def normal_values(own_key, dims, scale, limit, cuts=(), held_as=jnp.bfloat16):
    level = block_scale(own_key, dims, cuts, -0.22, 0.18) if cuts else 1.0
    values = jax.random.normal(own_key, dims, jnp.float32) * scale * level
    return jnp.minimum(jnp.maximum(values, -limit), limit).astype(held_as)


def setup_inputs(seed: int = 0, part: int = 0) -> dict:
    keys = jax.random.split(jax.random.key(seed), 15)
    own_keys = jax.random.split(jax.random.fold_in(keys[14], part), 15)
    return {
        "hidden": draw_hidden(jax.random.fold_in(jax.random.fold_in(keys[14], part), 71), part),
        "frame_cache": normal_values(own_keys[1], (1, 2, H, W, C), 1.0, 6.0, ((2, 4), (3, 4))),
        "shortcut": draw_shortcut(jax.random.fold_in(jax.random.fold_in(keys[14], part), 71), part),
        "gain_one": jnp.clip(jax.random.uniform(keys[3], (C,), jnp.float32, 0.5, 1.5), 0.5, 1.5),
        "conv_weight": normal_values(keys[4], (3, 3, 3, C, C), (27 * C) ** -0.5, 0.0625),
        "conv_bias": normal_values(keys[5], (C,), 0.3, 2.0, (), jnp.float32),
        "gain_two": jnp.clip(jax.random.uniform(keys[6], (C,), jnp.float32, 0.5, 1.5), 0.5, 1.5),
        "query_weight": draw_query_weight(jax.random.fold_in(keys[14], 71), part),
        "query_bias": normal_values(keys[8], (C,), 0.5, 3.0, (), jnp.float32),
        "key_weight": draw_key_weight(jax.random.fold_in(keys[14], 71), part),
        "value_weight": normal_values(keys[10], (C, C), C ** -0.5, 0.3125),
        "value_bias": normal_values(keys[11], (C,), 0.5, 3.0, (), jnp.float32),
        "out_weight": normal_values(keys[12], (C, C), C ** -0.5, 0.3125),
        "out_bias": normal_values(keys[13], (C,), 0.3, 2.0, (), jnp.float32),
    }


norm_epsilon = 1e-06

def rms_norm(field, gain):
    mean_square = lax.optimization_barrier(jnp.mean(field * field, axis=-1, keepdims=True))
    return field * lax.rsqrt(mean_square + norm_epsilon) * gain

def reference(hidden, frame_cache, shortcut, gain_one, conv_weight, conv_bias, gain_two, query_weight, query_bias, key_weight, value_weight, value_bias, out_weight, out_bias):
    current = hidden[0].astype(jnp.float32)
    activated = jax.nn.silu(rms_norm(current, gain_one)).astype(jnp.bfloat16)
    stacked = jnp.concatenate([frame_cache[0], activated[None]], axis=0).astype(jnp.float32)
    convolved = lax.conv_general_dilated(stacked[None], conv_weight.astype(jnp.float32), (1, 1, 1), [(0, 0), (1, 1), (1, 1)], dimension_numbers=('NDHWC', 'DHWIO', 'NDHWC'), precision=lax.Precision.HIGHEST)[0, 0] + conv_bias
    mixed = (shortcut[0].astype(jnp.float32) + convolved).astype(jnp.bfloat16)
    normed = rms_norm(mixed.astype(jnp.float32), gain_two).astype(jnp.bfloat16)
    flat_normed = normed.reshape(H * W, C)
    queries = (jnp.dot(flat_normed, query_weight, preferred_element_type=jnp.float32) + query_bias).astype(jnp.bfloat16)
    keys_all = jnp.dot(flat_normed, key_weight, preferred_element_type=jnp.float32).astype(jnp.bfloat16)
    values = (jnp.dot(flat_normed, value_weight, preferred_element_type=jnp.float32) + value_bias).astype(jnp.bfloat16)
    score_scale = float(C) ** (-0.5)

    def attend_block(query_block):
        scores = jnp.dot(query_block, keys_all.T, preferred_element_type=jnp.float32) * score_scale
        row_max = lax.optimization_barrier(jnp.max(scores, axis=1, keepdims=True))
        expos = jnp.exp(scores - row_max)
        probabilities = expos.astype(jnp.bfloat16)
        weighted = jnp.dot(probabilities, values, preferred_element_type=jnp.float32)
        return (weighted / lax.optimization_barrier(jnp.sum(expos, axis=1, keepdims=True))).astype(jnp.bfloat16)
    attended = lax.map(attend_block, queries.reshape(H, W, C)).reshape(H * W, C)
    projected = jnp.dot(attended, out_weight, preferred_element_type=jnp.float32) + out_bias
    decoded = (mixed.reshape(H * W, C).astype(jnp.float32) + projected).astype(jnp.bfloat16)
    return decoded.reshape(1, H, W, C)
```

```python
import functools

import jax
import jax.numpy as jnp
from jax import lax
from jax.experimental import pallas as pl
from jax.experimental.pallas import tpu as pltpu
from jax.sharding import PartitionSpec as P

norm_epsilon = 1e-06
stat_lanes = 128
f32 = jnp.float32
bf16 = jnp.bfloat16

VMEM = pl.BlockSpec(memory_space=pltpu.VMEM)
SMEM = pl.BlockSpec(memory_space=pltpu.SMEM)
ANY = pl.BlockSpec(memory_space=pl.ANY)


def near_pairs(count, first):
    pairs = []
    for i in range(first, count - 1, 2):
        pairs += [(i, i + 1), (i + 1, i)]
    return pairs


def far_pairs(count, step, stride=1):
    xor = count & (count - 1) == 0
    pairs = []
    for i in range(count):
        j = i ^ step if xor else (i + step) % count
        pairs += [(i * stride + k, j * stride + k) for k in range(stride)]
    return pairs


def normalize(cells, gain):
    mean_square = jnp.mean(cells * cells, axis=-1, keepdims=True)
    return cells * lax.rsqrt(mean_square + norm_epsilon) * gain


def activate(cells, gain):
    scaled = normalize(cells, gain)
    return scaled * (1.0 / (1.0 + jnp.exp(-scaled)))


def conv_kernel(
    tile_rows,
    tile_cols,
    channels,
    parity,
    cache,
    hidden,
    shortcut,
    row_a,
    row_b,
    col_a,
    col_b,
    gain_one,
    conv_bias,
    gain_two,
    weight,
    normed,
    mixed,
    held,
    stack,
    sems,
):
    copies = [
        pltpu.make_async_copy(weight.at[i], held.at[i], sems.at[i]) for i in range(9)
    ]
    for copy in copies:
        copy.start()
    row_even = parity[0] == 0
    col_even = parity[1] == 0
    place = lax.broadcasted_iota(jnp.int32, (tile_cols, channels), 0)
    reach = tile_rows + 2
    first = col_a[...].astype(f32)
    second = col_b[...].astype(f32)
    left_all = jnp.where(col_even, second, first)
    right_all = jnp.where(col_even, first, second)
    gain = gain_one[...]
    for f in range(3):
        left_rows = left_all[f * reach : (f + 1) * reach]
        right_rows = right_all[f * reach : (f + 1) * reach]
        if f == 2:
            left_rows = activate(left_rows, gain)
            right_rows = activate(right_rows, gain)
        for r in range(reach):
            if r == 0 or r == reach - 1:
                one, two = row_a[f].astype(f32), row_b[f].astype(f32)
                row = jnp.where(row_even, two, one) if r == 0 else jnp.where(row_even, one, two)
            elif f < 2:
                row = cache[0, f, r - 1].astype(f32)
            else:
                row = hidden[0, r - 1].astype(f32)
            if f == 2:
                row = activate(row, gain)
            from_left = jnp.where(place == 0, left_rows[r : r + 1], pltpu.roll(row, 1, 0))
            from_right = jnp.where(
                place == tile_cols - 1, right_rows[r : r + 1], pltpu.roll(row, tile_cols - 1, 0)
            )
            rows = pl.ds(r * tile_cols, tile_cols)
            stack[f, rows, 0:channels] = from_left.astype(bf16)
            stack[f, rows, channels : 2 * channels] = row.astype(bf16)
            stack[f, rows, 2 * channels : 3 * channels] = from_right.astype(bf16)
    total = jnp.zeros((tile_rows * tile_cols, channels), f32)
    for f in range(3):
        for a in range(3):
            copies[3 * f + a].wait()
            total += jnp.dot(
                stack[f, a * tile_cols : (a + tile_rows) * tile_cols, :],
                held[3 * f + a],
                preferred_element_type=f32,
            )
    convolved = total + conv_bias[...]
    residual = shortcut[...].astype(f32)
    kept = (residual + convolved).astype(bf16)
    mixed[...] = kept
    normed[...] = normalize(kept.astype(f32), gain_two[...]).astype(bf16)


def query_kernel(score_scale, parts, refs_in_out):
    sources = refs_in_out[:parts]
    query_weight, query_bias, key_weight, out = refs_in_out[parts:]
    at = 0
    for source in sources:
        rows = source.shape[0]
        queries = (
            jnp.dot(source[...], query_weight[...], preferred_element_type=f32) + query_bias[...]
        ).astype(bf16)
        turned = lax.dot_general(
            queries, key_weight[...], (((1,), (1,)), ((), ())), preferred_element_type=f32
        )
        out[at : at + rows] = (turned * score_scale).astype(bf16)
        at += rows


def pack(values, log_sum):
    lane = lax.broadcasted_iota(jnp.int32, (values.shape[0], stat_lanes), 1)
    high = log_sum.astype(bf16).astype(f32)
    rest = log_sum - high
    middle = rest.astype(bf16).astype(f32)
    low = rest - middle
    stats = jnp.where(
        lane == 0, high, jnp.where(lane == 1, middle, jnp.where(lane == 2, low, 0.0))
    )
    return values.astype(bf16), stats.astype(bf16)


def attend_kernel(blocks, kept_rows, chunk, *refs):
    queries = refs[0]
    keys = refs[1 : 1 + blocks]
    kept, kept_log, sent = refs[1 + blocks :]
    channels = queries.shape[1]
    for at in range(0, queries.shape[0], chunk):
        own = queries[at : at + chunk]
        scores = [
            lax.dot_general(own, key[...], (((1,), (1,)), ((), ())), preferred_element_type=f32)
            for key in keys
        ]
        top = functools.reduce(jnp.maximum, [jnp.max(s, axis=1, keepdims=True) for s in scores])
        expos = [jnp.exp(s - top) for s in scores]
        total = sum(jnp.sum(e, axis=1, keepdims=True) for e in expos)
        weighted = sum(
            jnp.dot(e.astype(bf16), key[...], preferred_element_type=f32)
            for e, key in zip(expos, keys)
        )
        mean = weighted / total
        log_sum = top + jnp.log(total)
        if at < kept_rows:
            kept[at : at + chunk] = mean
            kept_log[at : at + chunk] = jnp.broadcast_to(log_sum, (chunk, stat_lanes))
        else:
            to = at - kept_rows
            values, stats = pack(mean, log_sum)
            sent[to : to + chunk, 0:channels] = values
            sent[to : to + chunk, channels : channels + stat_lanes] = stats


def unpack(ref, rows):
    channels = ref.shape[1] - stat_lanes
    values = ref[rows, 0:channels].astype(f32)
    log_sum = jnp.sum(ref[rows, channels : channels + stat_lanes].astype(f32), axis=1, keepdims=True)
    return values, log_sum


def merge(parts):
    top = functools.reduce(jnp.maximum, [log_sum for _, log_sum in parts])
    scales = [jnp.exp(log_sum - top) for _, log_sum in parts]
    total = sum(scales)
    mean = sum(values * scale for (values, _), scale in zip(parts, scales)) / total
    return mean, top + jnp.log(total)


def chip_kernel(tile, kept, kept_log, received, own, own_log, *sent):
    for block in range(1 + len(sent)):
        rows = pl.ds(block * tile, tile)
        mean, log_sum = merge(
            [(kept[rows, :], kept_log[rows, 0:1]), unpack(received, rows)]
        )
        if block == 0:
            own[...] = mean
            own_log[...] = jnp.broadcast_to(log_sum, (tile, stat_lanes))
        else:
            channels = mean.shape[1]
            values, stats = pack(mean, log_sum)
            sent[block - 1][:, 0:channels] = values
            sent[block - 1][:, channels : channels + stat_lanes] = stats


def final_kernel(tile, others, *refs):
    own, own_log = refs[:2]
    received = refs[2 : 2 + others]
    mixed, value_weight, value_bias, out_weight, out_bias, decoded = refs[2 + others :]
    parts = [(own[...], own_log[:, 0:1])] + [unpack(ref, pl.ds(0, tile)) for ref in received]
    mean, _ = merge(parts)
    attended = (
        jnp.dot(mean.astype(bf16), value_weight[...], preferred_element_type=f32) + value_bias[...]
    ).astype(bf16)
    projected = jnp.dot(attended, out_weight[...], preferred_element_type=f32) + out_bias[...]
    decoded[...] = (mixed[...].astype(f32) + projected).astype(bf16)


def shape(dims, dtype):
    return jax.ShapeDtypeStruct(dims, dtype)


def per_device(
    hidden,
    frame_cache,
    shortcut,
    gain_one,
    conv_weight,
    conv_bias,
    gain_two,
    query_weight,
    query_bias,
    key_weight,
    value_weight,
    value_bias,
    out_weight,
    out_bias,
):
    _, tile_rows, tile_cols, channels = hidden.shape
    tile = tile_rows * tile_cols
    row_count, col_count = lax.axis_size("rows"), lax.axis_size("cols")
    chip_count = col_count // 2
    row_even = lax.axis_index("rows") % 2 == 0
    col_even = lax.axis_index("cols") % 2 == 0
    parity = jnp.stack([lax.axis_index("rows") % 2, lax.axis_index("cols") % 2]).astype(jnp.int32)
    row_vector = lambda v: v.reshape(1, channels)

    frames = jnp.concatenate([frame_cache[0], hidden], axis=0)
    top, bottom = frames[:, 0], frames[:, tile_rows - 1]
    row_a = lax.ppermute(jnp.where(row_even, bottom, top), "rows", near_pairs(row_count, 0))
    row_b = lax.ppermute(jnp.where(row_even, top, bottom), "rows", near_pairs(row_count, 1))
    above = jnp.where(row_even, row_b, row_a)
    below = jnp.where(row_even, row_a, row_b)
    edges = []
    for at in (0, tile_cols - 1):
        edges.append(
            jnp.concatenate(
                [above[:, at][:, None], frames[:, :, at], below[:, at][:, None]], axis=1
            ).reshape(3 * (tile_rows + 2), channels)
        )
    col_a = lax.ppermute(jnp.where(col_even, edges[1], edges[0]), "cols", near_pairs(col_count, 0))
    col_b = lax.ppermute(jnp.where(col_even, edges[0], edges[1]), "cols", near_pairs(col_count, 1))

    normed, mixed = pl.pallas_call(
        functools.partial(conv_kernel, tile_rows, tile_cols, channels),
        out_shape=(shape((tile, channels), bf16), shape((tile, channels), bf16)),
        in_specs=[SMEM] + [VMEM] * 10 + [ANY],
        out_specs=(VMEM, VMEM),
        scratch_shapes=[
            pltpu.VMEM((9, 3 * channels, channels), bf16),
            pltpu.VMEM((3, (tile_rows + 2) * tile_cols, 3 * channels), bf16),
            pltpu.SemaphoreType.DMA((9,)),
        ],
        name="conv",
    )(
        parity,
        frame_cache,
        hidden,
        shortcut.reshape(tile, channels),
        row_a,
        row_b,
        col_a,
        col_b,
        row_vector(gain_one),
        row_vector(conv_bias),
        row_vector(gain_two),
        conv_weight.reshape(9, 3 * channels, channels),
    )

    key_blocks = [normed] + [
        lax.ppermute(normed, "rows", far_pairs(row_count, step))
        for step in range(row_count - 1, 0, -1)
    ]
    query_blocks = jnp.concatenate(
        [normed]
        + [
            lax.ppermute(normed, "cols", far_pairs(chip_count, step, 2))
            for step in range(1, chip_count)
        ],
        axis=0,
    )
    other_queries = lax.ppermute(query_blocks, "cols", near_pairs(col_count, 0))
    query_rows = 2 * chip_count * tile
    queries = pl.pallas_call(
        lambda *refs: query_kernel(float(channels) ** (-0.5), 2, refs),
        out_shape=shape((query_rows, channels), bf16),
        in_specs=[VMEM] * 5,
        out_specs=VMEM,
        name="queries",
    )(query_blocks, other_queries, query_weight, row_vector(query_bias), key_weight)

    kept_rows = chip_count * tile
    kept, kept_log, sent = pl.pallas_call(
        functools.partial(attend_kernel, row_count, kept_rows, tile),
        out_shape=(
            shape((kept_rows, channels), f32),
            shape((kept_rows, stat_lanes), f32),
            shape((kept_rows, channels + stat_lanes), bf16),
        ),
        in_specs=[VMEM] * (1 + row_count),
        out_specs=(VMEM, VMEM, VMEM),
        name="attend",
    )(queries, *key_blocks)
    received = lax.ppermute(sent, "cols", near_pairs(col_count, 0))

    packed = shape((tile, channels + stat_lanes), bf16)
    own, own_log, *results = pl.pallas_call(
        functools.partial(chip_kernel, tile),
        out_shape=(shape((tile, channels), f32), shape((tile, stat_lanes), f32))
        + (packed,) * (chip_count - 1),
        in_specs=[VMEM] * 3,
        out_specs=(VMEM,) * (chip_count + 1),
        name="chip",
    )(kept, kept_log, received)
    returned = [
        lax.ppermute(
            result, "cols", [(j, i) for i, j in far_pairs(chip_count, step, 2)]
        )
        for step, result in enumerate(results, 1)
    ]
    decoded = pl.pallas_call(
        functools.partial(final_kernel, tile, chip_count - 1),
        out_shape=shape((tile, channels), bf16),
        in_specs=[VMEM] * (2 + chip_count - 1 + 5),
        out_specs=VMEM,
        name="final",
    )(
        own,
        own_log,
        *returned,
        mixed,
        value_weight,
        row_vector(value_bias),
        out_weight,
        row_vector(out_bias),
    )
    return decoded.reshape(1, tile_rows, tile_cols, channels)


def solution(mesh):
    placed = (
        P("videos", "rows", "cols", None),
        P("videos", None, "rows", "cols", None),
        P("videos", "rows", "cols", None),
        P(),
        P(),
        P(),
        P(),
        P(),
        P(),
        P(),
        P(),
        P(),
        P(),
        P(),
    )
    return jax.shard_map(
        per_device,
        mesh=mesh,
        in_specs=placed,
        out_specs=P("videos", "rows", "cols", None),
        check_vma=False,
    )
```

```python
import functools

import jax
import jax.numpy as jnp
from jax import lax
from jax.experimental import pallas as pl
from jax.experimental.pallas import tpu as pltpu
from jax.sharding import PartitionSpec as P


norm_epsilon = 1e-06
stat_lanes = 128
f32 = jnp.float32
bf16 = jnp.bfloat16

small_grant = 24 * 1024 * 1024
stage_cost = pl.CostEstimate(flops=10**10, bytes_accessed=10**7, transcendentals=0)
VMEM = pl.BlockSpec(memory_space=pltpu.VMEM)
SMEM = pl.BlockSpec(memory_space=pltpu.SMEM)
ANY = pl.BlockSpec(memory_space=pl.ANY)


def near_pairs(count, first):
    pairs = []
    for i in range(first, count - 1, 2):
        pairs += [(i, i + 1), (i + 1, i)]
    return pairs


def far_pairs(count, step, stride=1):
    xor = count & (count - 1) == 0
    pairs = []
    for i in range(count):
        j = i ^ step if xor else (i + step) % count
        pairs += [(i * stride + k, j * stride + k) for k in range(stride)]
    return pairs


def normalize(cells, gain):
    mean_square = jnp.mean(cells * cells, axis=-1, keepdims=True)
    return cells * lax.rsqrt(mean_square + norm_epsilon) * gain


def line(ref):
    return ref[...].reshape(1, ref.shape[0])


def activate(cells, gain):
    scaled = normalize(cells, gain)
    return scaled * (1.0 / (1.0 + jnp.exp(-scaled)))


def rows_kernel(tile_rows, cache, hidden, row_a, row_b, sems):
    odd = lax.rem(lax.axis_index("rows"), 2)
    copies = []
    for out, at in ((row_a, (1 - odd) * (tile_rows - 1)), (row_b, odd * (tile_rows - 1))):
        for f in range(3):
            source = cache.at[0, f, at] if f < 2 else hidden.at[0, at]
            copies.append(pltpu.make_async_copy(source, out.at[f], sems.at[len(copies)]))
    for copy in copies:
        copy.start()
    for copy in copies:
        copy.wait()


def cols_kernel(tile_rows, tile_cols, cache, hidden, row_a, row_b, col_a, col_b):
    row_even = lax.rem(lax.axis_index("rows"), 2) == 0
    col_even = lax.rem(lax.axis_index("cols"), 2) == 0
    first, last = pl.ds(0, 1), pl.ds(tile_cols - 1, 1)
    near, far = [], []

    def add(pick):
        left, right = pick(first).astype(f32), pick(last).astype(f32)
        near.append(jnp.where(col_even, right, left))
        far.append(jnp.where(col_even, left, right))

    for f in range(3):
        add(lambda at: jnp.where(row_even, row_b[f, at].astype(f32), row_a[f, at].astype(f32)))
        for r in range(tile_rows):
            add(lambda at: cache[0, f, r, at] if f < 2 else hidden[0, r, at])
        add(lambda at: jnp.where(row_even, row_a[f, at].astype(f32), row_b[f, at].astype(f32)))
    col_a[...] = jnp.concatenate(near, axis=0).astype(bf16)
    col_b[...] = jnp.concatenate(far, axis=0).astype(bf16)


def conv_kernel(
    tile_rows,
    tile_cols,
    channels,
    cache,
    hidden,
    shortcut,
    row_a,
    row_b,
    col_a,
    col_b,
    gain_one,
    conv_bias,
    gain_two,
    weight,
    normed,
    mixed,
    stack,
):
    row_even = lax.rem(lax.axis_index("rows"), 2) == 0
    col_even = lax.rem(lax.axis_index("cols"), 2) == 0
    place = lax.broadcasted_iota(jnp.int32, (tile_cols, channels), 0)
    reach = tile_rows + 2
    first = col_a[...].astype(f32)
    second = col_b[...].astype(f32)
    left_all = jnp.where(col_even, second, first)
    right_all = jnp.where(col_even, first, second)
    gain = line(gain_one)
    for f in range(3):
        left_rows = left_all[f * reach : (f + 1) * reach]
        right_rows = right_all[f * reach : (f + 1) * reach]
        if f == 2:
            left_rows = activate(left_rows, gain)
            right_rows = activate(right_rows, gain)
        for r in range(reach):
            if r == 0 or r == reach - 1:
                one, two = row_a[f].astype(f32), row_b[f].astype(f32)
                row = jnp.where(row_even, two, one) if r == 0 else jnp.where(row_even, one, two)
            elif f < 2:
                row = cache[0, f, r - 1].astype(f32)
            else:
                row = hidden[0, r - 1].astype(f32)
            if f == 2:
                row = activate(row, gain)
            from_left = jnp.where(place == 0, left_rows[r : r + 1], pltpu.roll(row, 1, 0))
            from_right = jnp.where(
                place == tile_cols - 1, right_rows[r : r + 1], pltpu.roll(row, tile_cols - 1, 0)
            )
            rows = pl.ds(r * tile_cols, tile_cols)
            stack[f, rows, 0:channels] = from_left.astype(bf16)
            stack[f, rows, channels : 2 * channels] = row.astype(bf16)
            stack[f, rows, 2 * channels : 3 * channels] = from_right.astype(bf16)
    total = jnp.zeros((tile_rows * tile_cols, channels), f32)
    for f in range(3):
        for a in range(3):
            total += jnp.dot(
                stack[f, a * tile_cols : (a + tile_rows) * tile_cols, :],
                weight[f, a].reshape(3 * channels, channels),
                preferred_element_type=f32,
            )
    convolved = total + line(conv_bias)
    residual = shortcut[...].astype(f32)
    kept = (residual + convolved).astype(bf16)
    mixed[...] = kept
    normed[...] = normalize(kept.astype(f32), line(gain_two)).astype(bf16)


def query_kernel(score_scale, parts, *refs):
    sources = refs[:parts]
    query_weight, query_bias, key_weight, out = refs[parts:]
    at = 0
    for source in sources:
        rows = source.shape[0]
        queries = (
            jnp.dot(source[...], query_weight[...], preferred_element_type=f32) + line(query_bias)
        ).astype(bf16)
        turned = lax.dot_general(
            queries, key_weight[...], (((1,), (1,)), ((), ())), preferred_element_type=f32
        )
        out[at : at + rows] = (turned * score_scale).astype(bf16)
        at += rows


def pack(values, log_sum):
    lane = lax.broadcasted_iota(jnp.int32, (values.shape[0], stat_lanes), 1)
    high = log_sum.astype(bf16).astype(f32)
    rest = log_sum - high
    middle = rest.astype(bf16).astype(f32)
    low = rest - middle
    stats = jnp.where(
        lane == 0, high, jnp.where(lane == 1, middle, jnp.where(lane == 2, low, 0.0))
    )
    return values.astype(bf16), stats.astype(bf16)


def attend_kernel(blocks, kept_rows, chunk, *refs):
    queries = refs[0]
    keys = refs[1 : 1 + blocks]
    kept, kept_log, sent = refs[1 + blocks :]
    channels = queries.shape[1]
    for at in range(0, queries.shape[0], chunk):
        own = queries[at : at + chunk]
        scores = [
            lax.dot_general(own, key[...], (((1,), (1,)), ((), ())), preferred_element_type=f32)
            for key in keys
        ]
        top = functools.reduce(jnp.maximum, [jnp.max(s, axis=1, keepdims=True) for s in scores])
        expos = [jnp.exp(s - top) for s in scores]
        total = sum(jnp.sum(e, axis=1, keepdims=True) for e in expos)
        weighted = sum(
            jnp.dot(e.astype(bf16), key[...], preferred_element_type=f32)
            for e, key in zip(expos, keys)
        )
        mean = weighted / total
        log_sum = top + jnp.log(total)
        if at < kept_rows:
            kept[at : at + chunk] = mean
            kept_log[at : at + chunk] = jnp.broadcast_to(log_sum, (chunk, stat_lanes))
        else:
            to = at - kept_rows
            values, stats = pack(mean, log_sum)
            sent[to : to + chunk, 0:channels] = values
            sent[to : to + chunk, channels : channels + stat_lanes] = stats


def unpack(ref, rows):
    channels = ref.shape[1] - stat_lanes
    values = ref[rows, 0:channels].astype(f32)
    log_sum = jnp.sum(ref[rows, channels : channels + stat_lanes].astype(f32), axis=1, keepdims=True)
    return values, log_sum


def merge(parts):
    top = functools.reduce(jnp.maximum, [log_sum for _, log_sum in parts])
    scales = [jnp.exp(log_sum - top) for _, log_sum in parts]
    total = sum(scales)
    mean = sum(values * scale for (values, _), scale in zip(parts, scales)) / total
    return mean, top + jnp.log(total)


def chip_kernel(tile, kept, kept_log, received, own, own_log, *sent):
    for block in range(1 + len(sent)):
        rows = pl.ds(block * tile, tile)
        mean, log_sum = merge(
            [(kept[rows, :], kept_log[rows, 0:1]), unpack(received, rows)]
        )
        if block == 0:
            own[...] = mean
            own_log[...] = jnp.broadcast_to(log_sum, (tile, stat_lanes))
        else:
            channels = mean.shape[1]
            values, stats = pack(mean, log_sum)
            sent[block - 1][:, 0:channels] = values
            sent[block - 1][:, channels : channels + stat_lanes] = stats


def final_kernel(tile, others, *refs):
    own, own_log = refs[:2]
    received = refs[2 : 2 + others]
    mixed, value_weight, value_bias, out_weight, out_bias, decoded = refs[2 + others :]
    parts = [(own[...], own_log[:, 0:1])] + [unpack(ref, pl.ds(0, tile)) for ref in received]
    mean, _ = merge(parts)
    attended = (
        jnp.dot(mean.astype(bf16), value_weight[...], preferred_element_type=f32) + line(value_bias)
    ).astype(bf16)
    projected = jnp.dot(attended, out_weight[...], preferred_element_type=f32) + line(out_bias)
    decoded[...] = (mixed[...].astype(f32) + projected).astype(bf16)


def call(kernel, out_shape, *operands, scratch_shapes=()):
    return pl.pallas_call(
        kernel,
        out_shape=out_shape,
        in_specs=[VMEM] * len(operands),
        out_specs=jax.tree.map(lambda _: VMEM, out_shape),
        scratch_shapes=scratch_shapes,
        compiler_params=pltpu.CompilerParams(vmem_limit_bytes=small_grant),
    )(*[pltpu.with_memory_space_constraint(operand, pltpu.VMEM) for operand in operands])


def per_device(
    hidden,
    frame_cache,
    shortcut,
    gain_one,
    conv_weight,
    conv_bias,
    gain_two,
    query_weight,
    query_bias,
    key_weight,
    value_weight,
    value_bias,
    out_weight,
    out_bias,
):
    _, tile_rows, tile_cols, channels = hidden.shape
    tile = tile_rows * tile_cols
    row_count, col_count = lax.axis_size("rows"), lax.axis_size("cols")
    chip_count = col_count // 2
    wide = pltpu.VMEM((tile, channels), bf16)

    edge_rows = pltpu.VMEM((3, tile_cols, channels), bf16)
    row_a, row_b = pl.pallas_call(
        functools.partial(rows_kernel, tile_rows),
        out_shape=(edge_rows, edge_rows),
        in_specs=[ANY, ANY],
        out_specs=(VMEM, VMEM),
        scratch_shapes=[pltpu.SemaphoreType.DMA((6,))],
        compiler_params=pltpu.CompilerParams(vmem_limit_bytes=small_grant),
        cost_estimate=stage_cost,
        name="edge_rows",
    )(*[pltpu.with_memory_space_constraint(v, pltpu.HBM) for v in (frame_cache, hidden)])
    row_a = lax.ppermute(row_a, "rows", near_pairs(row_count, 0))
    row_b = lax.ppermute(row_b, "rows", near_pairs(row_count, 1))
    edge_cols = pltpu.VMEM((3 * (tile_rows + 2), channels), bf16)
    col_a, col_b = call(
        functools.partial(cols_kernel, tile_rows, tile_cols),
        (edge_cols, edge_cols),
        frame_cache,
        hidden,
        row_a,
        row_b,
    )
    col_a = lax.ppermute(col_a, "cols", near_pairs(col_count, 0))
    col_b = lax.ppermute(col_b, "cols", near_pairs(col_count, 1))

    normed, mixed = call(
        functools.partial(conv_kernel, tile_rows, tile_cols, channels),
        (wide, wide),
        frame_cache,
        hidden,
        shortcut.reshape(tile, channels),
        row_a,
        row_b,
        col_a,
        col_b,
        gain_one,
        conv_bias,
        gain_two,
        conv_weight,
        scratch_shapes=[
            pltpu.VMEM((3, (tile_rows + 2) * tile_cols, 3 * channels), bf16),
        ],
    )

    key_blocks = [normed]
    for step in range(row_count - 1, 0, -1):
        key_blocks.append(lax.ppermute(normed, "rows", far_pairs(row_count, step)))
    near_queries = [normed]
    for step in range(1, chip_count):
        near_queries.append(lax.ppermute(normed, "cols", far_pairs(chip_count, step, 2)))
    other_queries = []
    for block in near_queries:
        other_queries.append(lax.ppermute(block, "cols", near_pairs(col_count, 0)))
    queries = call(
        functools.partial(query_kernel, float(channels) ** (-0.5), 2 * chip_count),
        pltpu.VMEM((2 * chip_count * tile, channels), bf16),
        *near_queries,
        *other_queries,
        query_weight,
        query_bias,
        key_weight,
    )

    kept_rows = chip_count * tile
    kept, kept_log, sent = call(
        functools.partial(attend_kernel, row_count, kept_rows, tile),
        (
            pltpu.VMEM((kept_rows, channels), f32),
            pltpu.VMEM((kept_rows, stat_lanes), f32),
            pltpu.VMEM((kept_rows, channels + stat_lanes), bf16),
        ),
        queries,
        *key_blocks,
    )
    received = lax.ppermute(sent, "cols", near_pairs(col_count, 0))

    packed = pltpu.VMEM((tile, channels + stat_lanes), bf16)
    own, own_log, *results = call(
        functools.partial(chip_kernel, tile),
        (pltpu.VMEM((tile, channels), f32), pltpu.VMEM((tile, stat_lanes), f32))
        + (packed,) * (chip_count - 1),
        kept,
        kept_log,
        received,
    )
    returned = [
        lax.ppermute(
            result, "cols", [(j, i) for i, j in far_pairs(chip_count, step, 2)]
        )
        for step, result in enumerate(results, 1)
    ]
    decoded = call(
        functools.partial(final_kernel, tile, chip_count - 1),
        jax.ShapeDtypeStruct((tile, channels), bf16),
        own,
        own_log,
        *returned,
        mixed,
        value_weight,
        value_bias,
        out_weight,
        out_bias,
    )
    return decoded.reshape(1, tile_rows, tile_cols, channels)


def solution(mesh):
    placed = (
        P("videos", "rows", "cols", None),
        P("videos", None, "rows", "cols", None),
        P("videos", "rows", "cols", None),
        P(),
        P(),
        P(),
        P(),
        P(),
        P(),
        P(),
        P(),
        P(),
        P(),
        P(),
    )
    return jax.shard_map(
        per_device,
        mesh=mesh,
        in_specs=placed,
        out_specs=P("videos", "rows", "cols", None),
        check_vma=False,
    )
```

```python
import functools

import jax
import jax.numpy as jnp
from jax import lax
from jax.experimental import pallas as pl
from jax.experimental.pallas import tpu as pltpu
from jax.sharding import PartitionSpec as P


norm_epsilon = 1e-06
stat_lanes = 128
f32 = jnp.float32
bf16 = jnp.bfloat16

small_grant = 24 * 1024 * 1024
stage_cost = pl.CostEstimate(flops=10**10, bytes_accessed=10**7, transcendentals=0)
VMEM = pl.BlockSpec(memory_space=pltpu.VMEM)
SMEM = pl.BlockSpec(memory_space=pltpu.SMEM)
ANY = pl.BlockSpec(memory_space=pl.ANY)


def near_pairs(count, first):
    pairs = []
    for i in range(first, count - 1, 2):
        pairs += [(i, i + 1), (i + 1, i)]
    return pairs


def far_pairs(count, step, stride=1):
    xor = count & (count - 1) == 0
    pairs = []
    for i in range(count):
        j = i ^ step if xor else (i + step) % count
        pairs += [(i * stride + k, j * stride + k) for k in range(stride)]
    return pairs


def normalize(cells, gain):
    mean_square = jnp.mean(cells * cells, axis=-1, keepdims=True)
    return cells * lax.rsqrt(mean_square + norm_epsilon) * gain


def line(ref):
    return ref[...].reshape(1, ref.shape[0])


def activate(cells, gain):
    scaled = normalize(cells, gain)
    return scaled * (1.0 / (1.0 + jnp.exp(-scaled)))


def rows_kernel(tile_rows, cache, hidden, row_a, row_b, sems):
    odd = lax.rem(lax.axis_index("rows"), 2)
    copies = []
    for out, at in ((row_a, (1 - odd) * (tile_rows - 1)), (row_b, odd * (tile_rows - 1))):
        for f in range(3):
            source = cache.at[0, f, at] if f < 2 else hidden.at[0, at]
            copies.append(pltpu.make_async_copy(source, out.at[f], sems.at[len(copies)]))
    for copy in copies:
        copy.start()
    for copy in copies:
        copy.wait()


def cols_kernel(tile_rows, tile_cols, cache, hidden, row_a, row_b, col_a, col_b):
    row_even = lax.rem(lax.axis_index("rows"), 2) == 0
    col_even = lax.rem(lax.axis_index("cols"), 2) == 0
    first, last = pl.ds(0, 1), pl.ds(tile_cols - 1, 1)
    near, far = [], []

    def add(pick):
        left, right = pick(first).astype(f32), pick(last).astype(f32)
        near.append(jnp.where(col_even, right, left))
        far.append(jnp.where(col_even, left, right))

    for f in range(3):
        add(lambda at: jnp.where(row_even, row_b[f, at].astype(f32), row_a[f, at].astype(f32)))
        for r in range(tile_rows):
            add(lambda at: cache[0, f, r, at] if f < 2 else hidden[0, r, at])
        add(lambda at: jnp.where(row_even, row_a[f, at].astype(f32), row_b[f, at].astype(f32)))
    col_a[...] = jnp.concatenate(near, axis=0).astype(bf16)
    col_b[...] = jnp.concatenate(far, axis=0).astype(bf16)


def conv_kernel(
    tile_rows,
    tile_cols,
    channels,
    cache,
    hidden,
    shortcut,
    row_a,
    row_b,
    col_a,
    col_b,
    gain_one,
    conv_bias,
    gain_two,
    weight,
    normed,
    mixed,
    stack,
):
    row_even = lax.rem(lax.axis_index("rows"), 2) == 0
    col_even = lax.rem(lax.axis_index("cols"), 2) == 0
    place = lax.broadcasted_iota(jnp.int32, (tile_cols, channels), 0)
    reach = tile_rows + 2
    first = col_a[...].astype(f32)
    second = col_b[...].astype(f32)
    left_all = jnp.where(col_even, second, first)
    right_all = jnp.where(col_even, first, second)
    gain = line(gain_one)
    for f in range(3):
        left_rows = left_all[f * reach : (f + 1) * reach]
        right_rows = right_all[f * reach : (f + 1) * reach]
        if f == 2:
            left_rows = activate(left_rows, gain)
            right_rows = activate(right_rows, gain)
        for r in range(reach):
            if r == 0 or r == reach - 1:
                one, two = row_a[f].astype(f32), row_b[f].astype(f32)
                row = jnp.where(row_even, two, one) if r == 0 else jnp.where(row_even, one, two)
            elif f < 2:
                row = cache[0, f, r - 1].astype(f32)
            else:
                row = hidden[0, r - 1].astype(f32)
            if f == 2:
                row = activate(row, gain)
            from_left = jnp.where(place == 0, left_rows[r : r + 1], pltpu.roll(row, 1, 0))
            from_right = jnp.where(
                place == tile_cols - 1, right_rows[r : r + 1], pltpu.roll(row, tile_cols - 1, 0)
            )
            rows = pl.ds(r * tile_cols, tile_cols)
            stack[f, rows, 0:channels] = from_left.astype(bf16)
            stack[f, rows, channels : 2 * channels] = row.astype(bf16)
            stack[f, rows, 2 * channels : 3 * channels] = from_right.astype(bf16)
    total = jnp.zeros((tile_rows * tile_cols, channels), f32)
    for f in range(3):
        for a in range(3):
            total += jnp.dot(
                stack[f, a * tile_cols : (a + tile_rows) * tile_cols, :],
                weight[f, a].reshape(3 * channels, channels),
                preferred_element_type=f32,
            )
    convolved = total + line(conv_bias)
    residual = shortcut[...].astype(f32)
    kept = (residual + convolved).astype(bf16)
    mixed[...] = kept
    normed[...] = normalize(kept.astype(f32), line(gain_two)).astype(bf16)


def query_kernel(score_scale, parts, *refs):
    sources = refs[:parts]
    query_weight, query_bias, key_weight, out = refs[parts:]
    at = 0
    for source in sources:
        rows = source.shape[0]
        queries = (
            jnp.dot(source[...], query_weight[...], preferred_element_type=f32) + line(query_bias)
        ).astype(bf16)
        turned = lax.dot_general(
            queries, key_weight[...], (((1,), (1,)), ((), ())), preferred_element_type=f32
        )
        out[at : at + rows] = (turned * score_scale).astype(bf16)
        at += rows


def pack(values, log_sum):
    lane = lax.broadcasted_iota(jnp.int32, (values.shape[0], stat_lanes), 1)
    high = log_sum.astype(bf16).astype(f32)
    rest = log_sum - high
    middle = rest.astype(bf16).astype(f32)
    low = rest - middle
    stats = jnp.where(
        lane == 0, high, jnp.where(lane == 1, middle, jnp.where(lane == 2, low, 0.0))
    )
    return values.astype(bf16), stats.astype(bf16)


def weigh(own, keys, state=None):
    scores = [
        lax.dot_general(own, key[...], (((1,), (1,)), ((), ())), preferred_element_type=f32)
        for key in keys
    ]
    tops = [jnp.max(s, axis=1, keepdims=True) for s in scores]
    top = functools.reduce(jnp.maximum, tops if state is None else tops + [state[0]])
    expos = [jnp.exp(s - top) for s in scores]
    total = sum(jnp.sum(e, axis=1, keepdims=True) for e in expos)
    weighted = sum(
        jnp.dot(e.astype(bf16), key[...], preferred_element_type=f32)
        for e, key in zip(expos, keys)
    )
    if state is not None:
        scale = jnp.exp(state[0] - top)
        total += state[1] * scale
        weighted += state[2] * scale
    return top, total, weighted


def early_kernel(tile, blocks, *refs):
    queries, keys = refs[0], refs[1 : 1 + blocks]
    tops, totals, weights = refs[1 + blocks :]
    for at in range(0, queries.shape[0], tile):
        rows = pl.ds(at, tile)
        top, total, weighted = weigh(queries[rows, :], keys)
        tops[rows, :] = jnp.broadcast_to(top, (tile, stat_lanes))
        totals[rows, :] = jnp.broadcast_to(total, (tile, stat_lanes))
        weights[rows, :] = weighted


def late_kernel(tile, blocks, first, *refs):
    queries, tops, totals, weights = refs[:4]
    keys, outs = refs[4 : 4 + blocks], list(refs[4 + blocks :])
    channels = queries.shape[1]
    block = first
    while outs:
        rows = pl.ds(block * tile, tile)
        state = (tops[rows, 0:1], totals[rows, 0:1], weights[rows, :])
        top, total, weighted = weigh(queries[rows, :], keys, state)
        mean, log_sum = weighted / total, top + jnp.log(total)
        if block == 0:
            own, own_log = outs.pop(0), outs.pop(0)
            own[...] = mean
            own_log[...] = jnp.broadcast_to(log_sum, (tile, stat_lanes))
        else:
            out = outs.pop(0)
            values, stats = pack(mean, log_sum)
            out[:, 0:channels] = values
            out[:, channels : channels + stat_lanes] = stats
        block += 1


def unpack(ref, rows):
    channels = ref.shape[1] - stat_lanes
    values = ref[rows, 0:channels].astype(f32)
    log_sum = jnp.sum(ref[rows, channels : channels + stat_lanes].astype(f32), axis=1, keepdims=True)
    return values, log_sum


def merge(parts):
    top = functools.reduce(jnp.maximum, [log_sum for _, log_sum in parts])
    scales = [jnp.exp(log_sum - top) for _, log_sum in parts]
    total = sum(scales)
    mean = sum(values * scale for (values, _), scale in zip(parts, scales)) / total
    return mean, top + jnp.log(total)


def final_kernel(tile, others, *refs):
    own, own_log = refs[:2]
    received = refs[2 : 2 + others]
    mixed, value_weight, value_bias, out_weight, out_bias, decoded = refs[2 + others :]
    parts = [(own[...], own_log[:, 0:1])] + [unpack(ref, pl.ds(0, tile)) for ref in received]
    mean, _ = merge(parts)
    attended = (
        jnp.dot(mean.astype(bf16), value_weight[...], preferred_element_type=f32) + line(value_bias)
    ).astype(bf16)
    projected = jnp.dot(attended, out_weight[...], preferred_element_type=f32) + line(out_bias)
    decoded[...] = (mixed[...].astype(f32) + projected).astype(bf16)


def call(kernel, out_shape, *operands, scratch_shapes=()):
    return pl.pallas_call(
        kernel,
        out_shape=out_shape,
        in_specs=[VMEM] * len(operands),
        out_specs=jax.tree.map(lambda _: VMEM, out_shape),
        scratch_shapes=scratch_shapes,
        compiler_params=pltpu.CompilerParams(vmem_limit_bytes=small_grant),
    )(*[pltpu.with_memory_space_constraint(operand, pltpu.VMEM) for operand in operands])


def per_device(
    hidden,
    frame_cache,
    shortcut,
    gain_one,
    conv_weight,
    conv_bias,
    gain_two,
    query_weight,
    query_bias,
    key_weight,
    value_weight,
    value_bias,
    out_weight,
    out_bias,
):
    _, tile_rows, tile_cols, channels = hidden.shape
    tile = tile_rows * tile_cols
    row_count, col_count = lax.axis_size("rows"), lax.axis_size("cols")
    chip_count = col_count // 2
    wide = pltpu.VMEM((tile, channels), bf16)

    edge_rows = pltpu.VMEM((3, tile_cols, channels), bf16)
    row_a, row_b = pl.pallas_call(
        functools.partial(rows_kernel, tile_rows),
        out_shape=(edge_rows, edge_rows),
        in_specs=[ANY, ANY],
        out_specs=(VMEM, VMEM),
        scratch_shapes=[pltpu.SemaphoreType.DMA((6,))],
        compiler_params=pltpu.CompilerParams(vmem_limit_bytes=small_grant),
        cost_estimate=stage_cost,
        name="edge_rows",
    )(*[pltpu.with_memory_space_constraint(v, pltpu.HBM) for v in (frame_cache, hidden)])
    row_a = lax.ppermute(row_a, "rows", near_pairs(row_count, 0))
    row_b = lax.ppermute(row_b, "rows", near_pairs(row_count, 1))
    edge_cols = pltpu.VMEM((3 * (tile_rows + 2), channels), bf16)
    col_a, col_b = call(
        functools.partial(cols_kernel, tile_rows, tile_cols),
        (edge_cols, edge_cols),
        frame_cache,
        hidden,
        row_a,
        row_b,
    )
    col_a = lax.ppermute(col_a, "cols", near_pairs(col_count, 0))
    col_b = lax.ppermute(col_b, "cols", near_pairs(col_count, 1))

    normed, mixed = call(
        functools.partial(conv_kernel, tile_rows, tile_cols, channels),
        (wide, wide),
        frame_cache,
        hidden,
        shortcut.reshape(tile, channels),
        row_a,
        row_b,
        col_a,
        col_b,
        gain_one,
        conv_bias,
        gain_two,
        conv_weight,
        scratch_shapes=[
            pltpu.VMEM((3, (tile_rows + 2) * tile_cols, 3 * channels), bf16),
        ],
    )

    partners = near_pairs(col_count, 0)
    arrived = {0: normed}
    for step in range(row_count - 1, 0, -1):
        arrived[step] = lax.ppermute(normed, "rows", far_pairs(row_count, step))
    query_blocks = [normed]
    for step in range(1, chip_count):
        query_blocks.append(lax.ppermute(normed, "cols", far_pairs(chip_count, step, 2)))
    keys = {}
    for step, block in arrived.items():
        keys[step] = [block, lax.ppermute(block, "cols", partners)]
    early = keys[0] + keys[row_count - 1]
    late = [key for step in range(1, row_count - 1) for key in keys[step]]

    query_rows = chip_count * tile
    queries = call(
        functools.partial(query_kernel, float(channels) ** (-0.5), chip_count),
        pltpu.VMEM((query_rows, channels), bf16),
        *query_blocks,
        query_weight,
        query_bias,
        key_weight,
    )
    stat = pltpu.VMEM((query_rows, stat_lanes), f32)
    state = call(
        functools.partial(early_kernel, tile, len(early)),
        (stat, stat, pltpu.VMEM((query_rows, channels), f32)),
        queries,
        *early,
    )
    packed = pltpu.VMEM((tile, channels + stat_lanes), bf16)
    results = call(
        functools.partial(late_kernel, tile, len(late), 1),
        (packed,) * (chip_count - 1),
        queries,
        *state,
        *late,
    )
    returned = []
    for step, result in enumerate(results, 1):
        returned.append(
            lax.ppermute(result, "cols", [(j, i) for i, j in far_pairs(chip_count, step, 2)])
        )
    own, own_log = call(
        functools.partial(late_kernel, tile, len(late), 0),
        (pltpu.VMEM((tile, channels), f32), pltpu.VMEM((tile, stat_lanes), f32)),
        queries,
        *state,
        *late,
    )
    decoded = call(
        functools.partial(final_kernel, tile, chip_count - 1),
        jax.ShapeDtypeStruct((tile, channels), bf16),
        own,
        own_log,
        *returned,
        mixed,
        value_weight,
        value_bias,
        out_weight,
        out_bias,
    )
    return decoded.reshape(1, tile_rows, tile_cols, channels)


def solution(mesh):
    placed = (
        P("videos", "rows", "cols", None),
        P("videos", None, "rows", "cols", None),
        P("videos", "rows", "cols", None),
        P(),
        P(),
        P(),
        P(),
        P(),
        P(),
        P(),
        P(),
        P(),
        P(),
        P(),
    )
    return jax.shard_map(
        per_device,
        mesh=mesh,
        in_specs=placed,
        out_specs=P("videos", "rows", "cols", None),
        check_vma=False,
    )
```

```python
import functools

import jax
import jax.numpy as jnp
from jax import lax
from jax.experimental import pallas as pl
from jax.experimental.pallas import tpu as pltpu
from jax.sharding import PartitionSpec as P


norm_epsilon = 1e-06
stat_lanes = 128
f32 = jnp.float32
bf16 = jnp.bfloat16

small_grant = 24 * 1024 * 1024
stage_cost = pl.CostEstimate(flops=10**10, bytes_accessed=10**7, transcendentals=0)
VMEM = pl.BlockSpec(memory_space=pltpu.VMEM)
SMEM = pl.BlockSpec(memory_space=pltpu.SMEM)
ANY = pl.BlockSpec(memory_space=pl.ANY)


def near_pairs(count, first):
    pairs = []
    for i in range(first, count - 1, 2):
        pairs += [(i, i + 1), (i + 1, i)]
    return pairs


def far_pairs(count, step, stride=1):
    xor = count & (count - 1) == 0
    pairs = []
    for i in range(count):
        j = i ^ step if xor else (i + step) % count
        pairs += [(i * stride + k, j * stride + k) for k in range(stride)]
    return pairs


def normalize(cells, gain):
    mean_square = jnp.mean(cells * cells, axis=-1, keepdims=True)
    return cells * lax.rsqrt(mean_square + norm_epsilon) * gain


def line(ref):
    return ref[...].reshape(1, ref.shape[0])


def activate(cells, gain):
    scaled = normalize(cells, gain)
    return scaled * (1.0 / (1.0 + jnp.exp(-scaled)))


def rows_kernel(tile_rows, cache, hidden, row_a, row_b, sems):
    odd = lax.rem(lax.axis_index("rows"), 2)
    copies = []
    for out, at in ((row_a, (1 - odd) * (tile_rows - 1)), (row_b, odd * (tile_rows - 1))):
        for f in range(3):
            source = cache.at[0, f, at] if f < 2 else hidden.at[0, at]
            copies.append(pltpu.make_async_copy(source, out.at[f], sems.at[len(copies)]))
    for copy in copies:
        copy.start()
    for copy in copies:
        copy.wait()


def cols_kernel(
    tile_rows, tile_cols, cache, hidden, row_a, row_b, gain_one, weight, inner, outer
):
    row_even = lax.rem(lax.axis_index("rows"), 2) == 0
    col_odd = lax.rem(lax.axis_index("cols"), 2)
    col_even = col_odd == 0
    first, last = pl.ds(0, 1), pl.ds(tile_cols - 1, 1)
    near, far = [], []

    def add(pick):
        left, right = pick(first).astype(f32), pick(last).astype(f32)
        near.append(jnp.where(col_even, right, left))
        far.append(jnp.where(col_even, left, right))

    for f in range(3):
        add(lambda at: jnp.where(row_even, row_b[f, at].astype(f32), row_a[f, at].astype(f32)))
        for r in range(tile_rows):
            add(lambda at: cache[0, f, r, at] if f < 2 else hidden[0, r, at])
        add(lambda at: jnp.where(row_even, row_a[f, at].astype(f32), row_b[f, at].astype(f32)))
    inner[...] = jnp.concatenate(near, axis=0).astype(bf16)
    reach = tile_rows + 2
    side = 2 - 2 * col_odd
    total = jnp.zeros((outer.shape[0], far[0].shape[1]), f32)
    spare = [jnp.zeros_like(far[0])] * (outer.shape[0] - tile_rows)
    for f in range(3):
        rows = far[f * reach : (f + 1) * reach]
        if f == 2:
            live = activate(jnp.concatenate(rows, axis=0), line(gain_one))
            rows = [live[r : r + 1] for r in range(reach)]
        for a in range(3):
            taken = jnp.concatenate(rows[a : a + tile_rows] + spare, axis=0).astype(bf16)
            total += jnp.dot(taken, weight[f, a, side], preferred_element_type=f32)
    outer[...] = total


def conv_kernel(
    tile_rows,
    tile_cols,
    channels,
    cache,
    hidden,
    row_a,
    row_b,
    inner,
    gain_one,
    weight,
    convolved,
    stack,
):
    row_even = lax.rem(lax.axis_index("rows"), 2) == 0
    col_even = lax.rem(lax.axis_index("cols"), 2) == 0
    place = lax.broadcasted_iota(jnp.int32, (tile_cols, channels), 0)
    reach = tile_rows + 2
    beside = inner[...].astype(f32)
    gain = line(gain_one)
    for f in range(3):
        side_rows = beside[f * reach : (f + 1) * reach]
        if f == 2:
            side_rows = activate(side_rows, gain)
        left_rows = jnp.where(col_even, 0.0, side_rows)
        right_rows = jnp.where(col_even, side_rows, 0.0)
        for r in range(reach):
            if r == 0 or r == reach - 1:
                one, two = row_a[f].astype(f32), row_b[f].astype(f32)
                row = jnp.where(row_even, two, one) if r == 0 else jnp.where(row_even, one, two)
            elif f < 2:
                row = cache[0, f, r - 1].astype(f32)
            else:
                row = hidden[0, r - 1].astype(f32)
            if f == 2:
                row = activate(row, gain)
            from_left = jnp.where(place == 0, left_rows[r : r + 1], pltpu.roll(row, 1, 0))
            from_right = jnp.where(
                place == tile_cols - 1, right_rows[r : r + 1], pltpu.roll(row, tile_cols - 1, 0)
            )
            rows = pl.ds(r * tile_cols, tile_cols)
            stack[f, rows, 0:channels] = from_left.astype(bf16)
            stack[f, rows, channels : 2 * channels] = row.astype(bf16)
            stack[f, rows, 2 * channels : 3 * channels] = from_right.astype(bf16)
    total = jnp.zeros((tile_rows * tile_cols, channels), f32)
    for f in range(3):
        for a in range(3):
            total += jnp.dot(
                stack[f, a * tile_cols : (a + tile_rows) * tile_cols, :],
                weight[f, a].reshape(3 * channels, channels),
                preferred_element_type=f32,
            )
    convolved[...] = total


def mix_kernel(
    tile_rows, tile_cols, convolved, outer, shortcut, conv_bias, gain_two, normed, mixed
):
    col_even = lax.rem(lax.axis_index("cols"), 2) == 0
    channels = shortcut.shape[-1]
    edge = jnp.where(col_even, 0, tile_cols - 1)
    place = lax.broadcasted_iota(jnp.int32, (tile_cols, channels), 0)
    bias, gain = line(conv_bias), line(gain_two)
    for r in range(tile_rows):
        rows = pl.ds(r * tile_cols, tile_cols)
        total = convolved[rows, :] + jnp.where(place == edge, outer[r : r + 1, :], 0.0)
        kept = (shortcut[0, r].astype(f32) + (total + bias)).astype(bf16)
        mixed[rows, :] = kept
        normed[rows, :] = normalize(kept.astype(f32), gain).astype(bf16)


def query_kernel(score_scale, parts, *refs):
    sources = refs[:parts]
    query_weight, query_bias, key_weight, out = refs[parts:]
    at = 0
    for source in sources:
        rows = source.shape[0]
        queries = (
            jnp.dot(source[...], query_weight[...], preferred_element_type=f32) + line(query_bias)
        ).astype(bf16)
        turned = lax.dot_general(
            queries, key_weight[...], (((1,), (1,)), ((), ())), preferred_element_type=f32
        )
        out[at : at + rows] = (turned * score_scale).astype(bf16)
        at += rows


def pack(values, log_sum):
    lane = lax.broadcasted_iota(jnp.int32, (values.shape[0], stat_lanes), 1)
    high = log_sum.astype(bf16).astype(f32)
    rest = log_sum - high
    middle = rest.astype(bf16).astype(f32)
    low = rest - middle
    stats = jnp.where(
        lane == 0, high, jnp.where(lane == 1, middle, jnp.where(lane == 2, low, 0.0))
    )
    return values.astype(bf16), stats.astype(bf16)


def weigh(own, keys, state=None):
    scores = [
        lax.dot_general(own, key[...], (((1,), (1,)), ((), ())), preferred_element_type=f32)
        for key in keys
    ]
    tops = [jnp.max(s, axis=1, keepdims=True) for s in scores]
    top = functools.reduce(jnp.maximum, tops if state is None else tops + [state[0]])
    expos = [jnp.exp(s - top) for s in scores]
    total = sum(jnp.sum(e, axis=1, keepdims=True) for e in expos)
    weighted = sum(
        jnp.dot(e.astype(bf16), key[...], preferred_element_type=f32)
        for e, key in zip(expos, keys)
    )
    if state is not None:
        scale = jnp.exp(state[0] - top)
        total += state[1] * scale
        weighted += state[2] * scale
    return top, total, weighted


def early_kernel(tile, blocks, *refs):
    queries, keys = refs[0], refs[1 : 1 + blocks]
    tops, totals, weights = refs[1 + blocks :]
    for at in range(0, queries.shape[0], tile):
        rows = pl.ds(at, tile)
        top, total, weighted = weigh(queries[rows, :], keys)
        tops[rows, :] = jnp.broadcast_to(top, (tile, stat_lanes))
        totals[rows, :] = jnp.broadcast_to(total, (tile, stat_lanes))
        weights[rows, :] = weighted


def late_kernel(tile, blocks, first, *refs):
    queries, tops, totals, weights = refs[:4]
    keys, outs = refs[4 : 4 + blocks], list(refs[4 + blocks :])
    channels = queries.shape[1]
    block = first
    while outs:
        rows = pl.ds(block * tile, tile)
        state = (tops[rows, 0:1], totals[rows, 0:1], weights[rows, :])
        top, total, weighted = weigh(queries[rows, :], keys, state)
        mean, log_sum = weighted / total, top + jnp.log(total)
        if block == 0:
            own, own_log = outs.pop(0), outs.pop(0)
            own[...] = mean
            own_log[...] = jnp.broadcast_to(log_sum, (tile, stat_lanes))
        else:
            out = outs.pop(0)
            values, stats = pack(mean, log_sum)
            out[:, 0:channels] = values
            out[:, channels : channels + stat_lanes] = stats
        block += 1


def unpack(ref, rows):
    channels = ref.shape[1] - stat_lanes
    values = ref[rows, 0:channels].astype(f32)
    log_sum = jnp.sum(ref[rows, channels : channels + stat_lanes].astype(f32), axis=1, keepdims=True)
    return values, log_sum


def merge(parts):
    top = functools.reduce(jnp.maximum, [log_sum for _, log_sum in parts])
    scales = [jnp.exp(log_sum - top) for _, log_sum in parts]
    total = sum(scales)
    mean = sum(values * scale for (values, _), scale in zip(parts, scales)) / total
    return mean, top + jnp.log(total)


def final_kernel(tile, others, *refs):
    own, own_log = refs[:2]
    received = refs[2 : 2 + others]
    mixed, value_weight, value_bias, out_weight, out_bias, decoded = refs[2 + others :]
    parts = [(own[...], own_log[:, 0:1])] + [unpack(ref, pl.ds(0, tile)) for ref in received]
    mean, _ = merge(parts)
    attended = (
        jnp.dot(mean.astype(bf16), value_weight[...], preferred_element_type=f32) + line(value_bias)
    ).astype(bf16)
    projected = jnp.dot(attended, out_weight[...], preferred_element_type=f32) + line(out_bias)
    decoded[...] = (mixed[...].astype(f32) + projected).astype(bf16)


def call(kernel, out_shape, *operands, scratch_shapes=()):
    return pl.pallas_call(
        kernel,
        out_shape=out_shape,
        in_specs=[VMEM] * len(operands),
        out_specs=jax.tree.map(lambda _: VMEM, out_shape),
        scratch_shapes=scratch_shapes,
        compiler_params=pltpu.CompilerParams(vmem_limit_bytes=small_grant),
    )(*[pltpu.with_memory_space_constraint(operand, pltpu.VMEM) for operand in operands])


def per_device(
    hidden,
    frame_cache,
    shortcut,
    gain_one,
    conv_weight,
    conv_bias,
    gain_two,
    query_weight,
    query_bias,
    key_weight,
    value_weight,
    value_bias,
    out_weight,
    out_bias,
):
    _, tile_rows, tile_cols, channels = hidden.shape
    tile = tile_rows * tile_cols
    row_count, col_count = lax.axis_size("rows"), lax.axis_size("cols")
    chip_count = col_count // 2
    wide = pltpu.VMEM((tile, channels), bf16)

    edge_rows = pltpu.VMEM((3, tile_cols, channels), bf16)
    row_a, row_b = pl.pallas_call(
        functools.partial(rows_kernel, tile_rows),
        out_shape=(edge_rows, edge_rows),
        in_specs=[ANY, ANY],
        out_specs=(VMEM, VMEM),
        scratch_shapes=[pltpu.SemaphoreType.DMA((6,))],
        compiler_params=pltpu.CompilerParams(vmem_limit_bytes=small_grant),
        cost_estimate=stage_cost,
        name="edge_rows",
    )(*[pltpu.with_memory_space_constraint(v, pltpu.HBM) for v in (frame_cache, hidden)])
    row_a = lax.ppermute(row_a, "rows", near_pairs(row_count, 0))
    row_b = lax.ppermute(row_b, "rows", near_pairs(row_count, 1))
    inner, outer = call(
        functools.partial(cols_kernel, tile_rows, tile_cols),
        (
            pltpu.VMEM((3 * (tile_rows + 2), channels), bf16),
            pltpu.VMEM((-(-tile_rows // 8) * 8, channels), f32),
        ),
        frame_cache,
        hidden,
        row_a,
        row_b,
        gain_one,
        conv_weight,
    )
    inner = lax.ppermute(inner, "cols", near_pairs(col_count, 0))
    outer = lax.ppermute(outer, "cols", near_pairs(col_count, 1))
    convolved = call(
        functools.partial(conv_kernel, tile_rows, tile_cols, channels),
        pltpu.VMEM((tile, channels), f32),
        frame_cache,
        hidden,
        row_a,
        row_b,
        inner,
        gain_one,
        conv_weight,
        scratch_shapes=[
            pltpu.VMEM((3, (tile_rows + 2) * tile_cols, 3 * channels), bf16),
        ],
    )
    normed, mixed = call(
        functools.partial(mix_kernel, tile_rows, tile_cols),
        (wide, wide),
        convolved,
        outer,
        shortcut,
        conv_bias,
        gain_two,
    )

    partners = near_pairs(col_count, 0)
    arrived = {0: normed}
    for step in range(row_count - 1, 0, -1):
        arrived[step] = lax.ppermute(normed, "rows", far_pairs(row_count, step))
    query_blocks = [normed]
    for step in range(1, chip_count):
        query_blocks.append(lax.ppermute(normed, "cols", far_pairs(chip_count, step, 2)))
    keys = {}
    for step, block in arrived.items():
        keys[step] = [block, lax.ppermute(block, "cols", partners)]
    early = keys[0] + keys[row_count - 1]
    late = [key for step in range(1, row_count - 1) for key in keys[step]]

    query_rows = chip_count * tile
    queries = call(
        functools.partial(query_kernel, float(channels) ** (-0.5), chip_count),
        pltpu.VMEM((query_rows, channels), bf16),
        *query_blocks,
        query_weight,
        query_bias,
        key_weight,
    )
    stat = pltpu.VMEM((query_rows, stat_lanes), f32)
    state = call(
        functools.partial(early_kernel, tile, len(early)),
        (stat, stat, pltpu.VMEM((query_rows, channels), f32)),
        queries,
        *early,
    )
    packed = pltpu.VMEM((tile, channels + stat_lanes), bf16)
    results = call(
        functools.partial(late_kernel, tile, len(late), 1),
        (packed,) * (chip_count - 1),
        queries,
        *state,
        *late,
    )
    returned = []
    for step, result in enumerate(results, 1):
        returned.append(
            lax.ppermute(result, "cols", [(j, i) for i, j in far_pairs(chip_count, step, 2)])
        )
    own, own_log = call(
        functools.partial(late_kernel, tile, len(late), 0),
        (pltpu.VMEM((tile, channels), f32), pltpu.VMEM((tile, stat_lanes), f32)),
        queries,
        *state,
        *late,
    )
    decoded = call(
        functools.partial(final_kernel, tile, chip_count - 1),
        jax.ShapeDtypeStruct((tile, channels), bf16),
        own,
        own_log,
        *returned,
        mixed,
        value_weight,
        value_bias,
        out_weight,
        out_bias,
    )
    return decoded.reshape(1, tile_rows, tile_cols, channels)


def solution(mesh):
    placed = (
        P("videos", "rows", "cols", None),
        P("videos", None, "rows", "cols", None),
        P("videos", "rows", "cols", None),
        P(),
        P(),
        P(),
        P(),
        P(),
        P(),
        P(),
        P(),
        P(),
        P(),
        P(),
    )
    return jax.shard_map(
        per_device,
        mesh=mesh,
        in_specs=placed,
        out_specs=P("videos", "rows", "cols", None),
        check_vma=False,
    )
```

```python
import functools

import jax
import jax.numpy as jnp
from jax import lax
from jax.experimental import pallas as pl
from jax.experimental.pallas import tpu as pltpu
from jax.sharding import PartitionSpec as P


norm_epsilon = 1e-06
stat_lanes = 128
stat_rows = 8
f32 = jnp.float32
bf16 = jnp.bfloat16

small_grant = 24 * 1024 * 1024
stage_cost = pl.CostEstimate(flops=10**10, bytes_accessed=10**7, transcendentals=0)
VMEM = pl.BlockSpec(memory_space=pltpu.VMEM)
SMEM = pl.BlockSpec(memory_space=pltpu.SMEM)
ANY = pl.BlockSpec(memory_space=pl.ANY)


def near_pairs(count, first):
    pairs = []
    for i in range(first, count - 1, 2):
        pairs += [(i, i + 1), (i + 1, i)]
    return pairs


def far_pairs(count, step, stride=1):
    xor = count & (count - 1) == 0
    pairs = []
    for i in range(count):
        j = i ^ step if xor else (i + step) % count
        pairs += [(i * stride + k, j * stride + k) for k in range(stride)]
    return pairs


def normalize(cells, gain):
    mean_square = jnp.mean(cells * cells, axis=-1, keepdims=True)
    return cells * lax.rsqrt(mean_square + norm_epsilon) * gain


def line(ref):
    return ref[...].reshape(1, ref.shape[0])


def activate(cells, gain):
    scaled = normalize(cells, gain)
    return scaled * (1.0 / (1.0 + jnp.exp(-scaled)))


def rows_kernel(tile_rows, cache, hidden, row_a, row_b, sems):
    odd = lax.rem(lax.axis_index("rows"), 2)
    copies = []
    for out, at in ((row_a, (1 - odd) * (tile_rows - 1)), (row_b, odd * (tile_rows - 1))):
        for f in range(3):
            source = cache.at[0, f, at] if f < 2 else hidden.at[0, at]
            copies.append(pltpu.make_async_copy(source, out.at[f], sems.at[len(copies)]))
    for copy in copies:
        copy.start()
    for copy in copies:
        copy.wait()


def cols_kernel(
    tile_rows, tile_cols, cache, hidden, row_a, row_b, gain_one, weight, inner, outer
):
    row_even = lax.rem(lax.axis_index("rows"), 2) == 0
    col_odd = lax.rem(lax.axis_index("cols"), 2)
    col_even = col_odd == 0
    first, last = pl.ds(0, 1), pl.ds(tile_cols - 1, 1)
    near, far = [], []

    def add(pick):
        left, right = pick(first).astype(f32), pick(last).astype(f32)
        near.append(jnp.where(col_even, right, left))
        far.append(jnp.where(col_even, left, right))

    for f in range(3):
        add(lambda at: jnp.where(row_even, row_b[f, at].astype(f32), row_a[f, at].astype(f32)))
        for r in range(tile_rows):
            add(lambda at: cache[0, f, r, at] if f < 2 else hidden[0, r, at])
        add(lambda at: jnp.where(row_even, row_a[f, at].astype(f32), row_b[f, at].astype(f32)))
    inner[...] = jnp.concatenate(near, axis=0).astype(bf16)
    reach = tile_rows + 2
    side = 2 - 2 * col_odd
    total = jnp.zeros((outer.shape[0], far[0].shape[1]), f32)
    spare = [jnp.zeros_like(far[0])] * (outer.shape[0] - tile_rows)
    for f in range(3):
        rows = far[f * reach : (f + 1) * reach]
        if f == 2:
            live = activate(jnp.concatenate(rows, axis=0), line(gain_one))
            rows = [live[r : r + 1] for r in range(reach)]
        for a in range(3):
            taken = jnp.concatenate(rows[a : a + tile_rows] + spare, axis=0).astype(bf16)
            total += jnp.dot(taken, weight[f, a, side], preferred_element_type=f32)
    outer[...] = total


def conv_kernel(
    tile_rows,
    tile_cols,
    channels,
    cache,
    hidden,
    row_a,
    row_b,
    inner,
    gain_one,
    weight,
    convolved,
    stack,
):
    row_even = lax.rem(lax.axis_index("rows"), 2) == 0
    col_even = lax.rem(lax.axis_index("cols"), 2) == 0
    place = lax.broadcasted_iota(jnp.int32, (tile_cols, channels), 0)
    reach = tile_rows + 2
    beside = inner[...].astype(f32)
    gain = line(gain_one)
    for f in range(3):
        side_rows = beside[f * reach : (f + 1) * reach]
        if f == 2:
            side_rows = activate(side_rows, gain)
        left_rows = jnp.where(col_even, 0.0, side_rows)
        right_rows = jnp.where(col_even, side_rows, 0.0)
        for r in range(reach):
            if r == 0 or r == reach - 1:
                one, two = row_a[f].astype(f32), row_b[f].astype(f32)
                row = jnp.where(row_even, two, one) if r == 0 else jnp.where(row_even, one, two)
            elif f < 2:
                row = cache[0, f, r - 1].astype(f32)
            else:
                row = hidden[0, r - 1].astype(f32)
            if f == 2:
                row = activate(row, gain)
            from_left = jnp.where(place == 0, left_rows[r : r + 1], pltpu.roll(row, 1, 0))
            from_right = jnp.where(
                place == tile_cols - 1, right_rows[r : r + 1], pltpu.roll(row, tile_cols - 1, 0)
            )
            rows = pl.ds(r * tile_cols, tile_cols)
            stack[f, rows, 0:channels] = from_left.astype(bf16)
            stack[f, rows, channels : 2 * channels] = row.astype(bf16)
            stack[f, rows, 2 * channels : 3 * channels] = from_right.astype(bf16)
    total = jnp.zeros((tile_rows * tile_cols, channels), f32)
    for f in range(3):
        for a in range(3):
            total += jnp.dot(
                stack[f, a * tile_cols : (a + tile_rows) * tile_cols, :],
                weight[f, a].reshape(3 * channels, channels),
                preferred_element_type=f32,
            )
    convolved[...] = total


def mix_kernel(
    tile_rows, tile_cols, convolved, outer, shortcut, conv_bias, gain_two, normed, mixed
):
    col_even = lax.rem(lax.axis_index("cols"), 2) == 0
    channels = shortcut.shape[-1]
    edge = jnp.where(col_even, 0, tile_cols - 1)
    place = lax.broadcasted_iota(jnp.int32, (tile_cols, channels), 0)
    bias, gain = line(conv_bias), line(gain_two)
    for r in range(tile_rows):
        rows = pl.ds(r * tile_cols, tile_cols)
        total = convolved[rows, :] + jnp.where(place == edge, outer[r : r + 1, :], 0.0)
        kept = (shortcut[0, r].astype(f32) + (total + bias)).astype(bf16)
        mixed[rows, :] = kept
        normed[rows, :] = normalize(kept.astype(f32), gain).astype(bf16)


def query_kernel(score_scale, parts, *refs):
    sources = refs[:parts]
    query_weight, query_bias, key_weight, out = refs[parts:]
    at = 0
    for source in sources:
        rows = source.shape[0]
        queries = (
            jnp.dot(source[...], query_weight[...], preferred_element_type=f32) + line(query_bias)
        ).astype(bf16)
        turned = lax.dot_general(
            queries, key_weight[...], (((1,), (1,)), ((), ())), preferred_element_type=f32
        )
        out[at : at + rows] = (turned * score_scale).astype(bf16)
        at += rows


def pack(out, values, log_sum):
    count, channels = values.shape
    lane = lax.broadcasted_iota(jnp.int32, (count, stat_lanes), 1)
    high = log_sum.astype(bf16).astype(f32)
    rest = log_sum - high
    middle = rest.astype(bf16).astype(f32)
    low = rest - middle
    stats = jnp.where(
        lane == 0, high, jnp.where(lane == 1, middle, jnp.where(lane == 2, low, 0.0))
    )
    out[0:count, :] = values.astype(bf16)
    flat = jnp.transpose(stats)[0:stat_rows, :]
    fill = jnp.zeros((stat_rows, channels - count), f32)
    out[count : count + stat_rows, :] = jnp.concatenate([flat, fill], axis=1).astype(bf16)


def weigh(own, keys, state=None):
    scores = [
        lax.dot_general(own, key[...], (((1,), (1,)), ((), ())), preferred_element_type=f32)
        for key in keys
    ]
    tops = [jnp.max(s, axis=1, keepdims=True) for s in scores]
    top = functools.reduce(jnp.maximum, tops if state is None else tops + [state[0]])
    expos = [jnp.exp(s - top) for s in scores]
    total = sum(jnp.sum(e, axis=1, keepdims=True) for e in expos)
    weighted = sum(
        jnp.dot(e.astype(bf16), key[...], preferred_element_type=f32)
        for e, key in zip(expos, keys)
    )
    if state is not None:
        scale = jnp.exp(state[0] - top)
        total += state[1] * scale
        weighted += state[2] * scale
    return top, total, weighted


def early_kernel(tile, blocks, *refs):
    queries, keys = refs[0], refs[1 : 1 + blocks]
    tops, totals, weights = refs[1 + blocks :]
    for at in range(0, queries.shape[0], tile):
        rows = pl.ds(at, tile)
        top, total, weighted = weigh(queries[rows, :], keys)
        tops[rows, :] = jnp.broadcast_to(top, (tile, stat_lanes))
        totals[rows, :] = jnp.broadcast_to(total, (tile, stat_lanes))
        weights[rows, :] = weighted


def late_kernel(tile, blocks, first, *refs):
    queries, tops, totals, weights = refs[:4]
    keys, outs = refs[4 : 4 + blocks], list(refs[4 + blocks :])
    block = first
    while outs:
        rows = pl.ds(block * tile, tile)
        state = (tops[rows, 0:1], totals[rows, 0:1], weights[rows, :])
        top, total, weighted = weigh(queries[rows, :], keys, state)
        mean, log_sum = weighted / total, top + jnp.log(total)
        if block == 0:
            own, own_log = outs.pop(0), outs.pop(0)
            own[...] = mean
            own_log[...] = jnp.broadcast_to(log_sum, (tile, stat_lanes))
        else:
            pack(outs.pop(0), mean, log_sum)
        block += 1


def unpack(ref, count):
    flat = ref[count : count + stat_rows, 0:count].astype(f32)
    stats = jnp.transpose(jnp.concatenate([flat] * (stat_lanes // stat_rows), axis=0))
    return ref[0:count, :].astype(f32), jnp.sum(stats[:, 0:3], axis=1, keepdims=True)


def merge(parts):
    top = functools.reduce(jnp.maximum, [log_sum for _, log_sum in parts])
    scales = [jnp.exp(log_sum - top) for _, log_sum in parts]
    total = sum(scales)
    mean = sum(values * scale for (values, _), scale in zip(parts, scales)) / total
    return mean, top + jnp.log(total)


def final_kernel(tile, others, *refs):
    own, own_log = refs[:2]
    received = refs[2 : 2 + others]
    mixed, value_weight, value_bias, out_weight, out_bias, decoded = refs[2 + others :]
    parts = [(own[...], own_log[:, 0:1])] + [unpack(ref, tile) for ref in received]
    mean, _ = merge(parts)
    attended = (
        jnp.dot(mean.astype(bf16), value_weight[...], preferred_element_type=f32) + line(value_bias)
    ).astype(bf16)
    projected = jnp.dot(attended, out_weight[...], preferred_element_type=f32) + line(out_bias)
    decoded[...] = (mixed[...].astype(f32) + projected).astype(bf16)


def call(kernel, out_shape, *operands, scratch_shapes=()):
    return pl.pallas_call(
        kernel,
        out_shape=out_shape,
        in_specs=[VMEM] * len(operands),
        out_specs=jax.tree.map(lambda _: VMEM, out_shape),
        scratch_shapes=scratch_shapes,
        compiler_params=pltpu.CompilerParams(vmem_limit_bytes=small_grant),
    )(*[pltpu.with_memory_space_constraint(operand, pltpu.VMEM) for operand in operands])


def per_device(
    hidden,
    frame_cache,
    shortcut,
    gain_one,
    conv_weight,
    conv_bias,
    gain_two,
    query_weight,
    query_bias,
    key_weight,
    value_weight,
    value_bias,
    out_weight,
    out_bias,
):
    _, tile_rows, tile_cols, channels = hidden.shape
    tile = tile_rows * tile_cols
    row_count, col_count = lax.axis_size("rows"), lax.axis_size("cols")
    chip_count = col_count // 2
    wide = pltpu.VMEM((tile, channels), bf16)

    edge_rows = pltpu.VMEM((3, tile_cols, channels), bf16)
    row_a, row_b = pl.pallas_call(
        functools.partial(rows_kernel, tile_rows),
        out_shape=(edge_rows, edge_rows),
        in_specs=[ANY, ANY],
        out_specs=(VMEM, VMEM),
        scratch_shapes=[pltpu.SemaphoreType.DMA((6,))],
        compiler_params=pltpu.CompilerParams(vmem_limit_bytes=small_grant),
        cost_estimate=stage_cost,
        name="edge_rows",
    )(*[pltpu.with_memory_space_constraint(v, pltpu.HBM) for v in (frame_cache, hidden)])
    row_a = lax.ppermute(row_a, "rows", near_pairs(row_count, 0))
    row_b = lax.ppermute(row_b, "rows", near_pairs(row_count, 1))
    inner, outer = call(
        functools.partial(cols_kernel, tile_rows, tile_cols),
        (
            pltpu.VMEM((3 * (tile_rows + 2), channels), bf16),
            pltpu.VMEM((-(-tile_rows // 8) * 8, channels), f32),
        ),
        frame_cache,
        hidden,
        row_a,
        row_b,
        gain_one,
        conv_weight,
    )
    inner = lax.ppermute(inner, "cols", near_pairs(col_count, 0))
    outer = lax.ppermute(outer, "cols", near_pairs(col_count, 1))
    convolved = call(
        functools.partial(conv_kernel, tile_rows, tile_cols, channels),
        pltpu.VMEM((tile, channels), f32),
        frame_cache,
        hidden,
        row_a,
        row_b,
        inner,
        gain_one,
        conv_weight,
        scratch_shapes=[
            pltpu.VMEM((3, (tile_rows + 2) * tile_cols, 3 * channels), bf16),
        ],
    )
    normed, mixed = call(
        functools.partial(mix_kernel, tile_rows, tile_cols),
        (wide, wide),
        convolved,
        outer,
        shortcut,
        conv_bias,
        gain_two,
    )

    partners = near_pairs(col_count, 0)
    arrived = {0: normed}
    for step in range(row_count - 1, 0, -1):
        arrived[step] = lax.ppermute(normed, "rows", far_pairs(row_count, step))
    query_blocks = [normed]
    for step in range(1, chip_count):
        query_blocks.append(lax.ppermute(normed, "cols", far_pairs(chip_count, step, 2)))
    keys = {}
    for step, block in arrived.items():
        keys[step] = [block, lax.ppermute(block, "cols", partners)]
    early = keys[0] + keys[row_count - 1]
    late = [key for step in range(1, row_count - 1) for key in keys[step]]

    query_rows = chip_count * tile
    queries = call(
        functools.partial(query_kernel, float(channels) ** (-0.5), chip_count),
        pltpu.VMEM((query_rows, channels), bf16),
        *query_blocks,
        query_weight,
        query_bias,
        key_weight,
    )
    stat = pltpu.VMEM((query_rows, stat_lanes), f32)
    state = call(
        functools.partial(early_kernel, tile, len(early)),
        (stat, stat, pltpu.VMEM((query_rows, channels), f32)),
        queries,
        *early,
    )
    packed = pltpu.VMEM((tile + stat_rows, channels), bf16)
    results = call(
        functools.partial(late_kernel, tile, len(late), 1),
        (packed,) * (chip_count - 1),
        queries,
        *state,
        *late,
    )
    returned = []
    for step, result in enumerate(results, 1):
        returned.append(
            lax.ppermute(result, "cols", [(j, i) for i, j in far_pairs(chip_count, step, 2)])
        )
    own, own_log = call(
        functools.partial(late_kernel, tile, len(late), 0),
        (pltpu.VMEM((tile, channels), f32), pltpu.VMEM((tile, stat_lanes), f32)),
        queries,
        *state,
        *late,
    )
    decoded = call(
        functools.partial(final_kernel, tile, chip_count - 1),
        jax.ShapeDtypeStruct((tile, channels), bf16),
        own,
        own_log,
        *returned,
        mixed,
        value_weight,
        value_bias,
        out_weight,
        out_bias,
    )
    return decoded.reshape(1, tile_rows, tile_cols, channels)


def solution(mesh):
    placed = (
        P("videos", "rows", "cols", None),
        P("videos", None, "rows", "cols", None),
        P("videos", "rows", "cols", None),
        P(),
        P(),
        P(),
        P(),
        P(),
        P(),
        P(),
        P(),
        P(),
        P(),
        P(),
    )
    return jax.shard_map(
        per_device,
        mesh=mesh,
        in_specs=placed,
        out_specs=P("videos", "rows", "cols", None),
        check_vma=False,
    )
```

```python
import functools

import jax
import jax.numpy as jnp
from jax import lax
from jax.experimental import pallas as pl
from jax.experimental.pallas import tpu as pltpu
from jax.sharding import PartitionSpec as P


norm_epsilon = 1e-06
stat_lanes = 128
stat_rows = 8
f32 = jnp.float32
bf16 = jnp.bfloat16

small_grant = 24 * 1024 * 1024
stage_cost = pl.CostEstimate(flops=10**10, bytes_accessed=10**7, transcendentals=0)
VMEM = pl.BlockSpec(memory_space=pltpu.VMEM)
SMEM = pl.BlockSpec(memory_space=pltpu.SMEM)
ANY = pl.BlockSpec(memory_space=pl.ANY)


def near_pairs(count, first):
    pairs = []
    for i in range(first, count - 1, 2):
        pairs += [(i, i + 1), (i + 1, i)]
    return pairs


def far_pairs(count, step, stride=1):
    xor = count & (count - 1) == 0
    pairs = []
    for i in range(count):
        j = i ^ step if xor else (i + step) % count
        pairs += [(i * stride + k, j * stride + k) for k in range(stride)]
    return pairs


def normalize(cells, gain):
    mean_square = jnp.mean(cells * cells, axis=-1, keepdims=True)
    return cells * lax.rsqrt(mean_square + norm_epsilon) * gain


def line(ref):
    return ref[...].reshape(1, ref.shape[0])


def activate(cells, gain):
    scaled = normalize(cells, gain)
    return scaled * (1.0 / (1.0 + jnp.exp(-scaled)))


def rows_kernel(tile_rows, cache, hidden, row_a, row_b, sems):
    odd = lax.rem(lax.axis_index("rows"), 2)
    copies = []
    for out, at in ((row_a, (1 - odd) * (tile_rows - 1)), (row_b, odd * (tile_rows - 1))):
        for f in range(3):
            source = cache.at[0, f, at] if f < 2 else hidden.at[0, at]
            copies.append(pltpu.make_async_copy(source, out.at[f], sems.at[len(copies)]))
    for copy in copies:
        copy.start()
    for copy in copies:
        copy.wait()


def cols_kernel(
    tile_rows, tile_cols, cache, hidden, row_a, row_b, gain_one, weight, inner, outer
):
    row_even = lax.rem(lax.axis_index("rows"), 2) == 0
    col_odd = lax.rem(lax.axis_index("cols"), 2)
    col_even = col_odd == 0
    first, last = pl.ds(0, 1), pl.ds(tile_cols - 1, 1)
    near, far = [], []

    def add(pick):
        left, right = pick(first).astype(f32), pick(last).astype(f32)
        near.append(jnp.where(col_even, right, left))
        far.append(jnp.where(col_even, left, right))

    for f in range(3):
        add(lambda at: jnp.where(row_even, row_b[f, at].astype(f32), row_a[f, at].astype(f32)))
        for r in range(tile_rows):
            add(lambda at: cache[0, f, r, at] if f < 2 else hidden[0, r, at])
        add(lambda at: jnp.where(row_even, row_a[f, at].astype(f32), row_b[f, at].astype(f32)))
    inner[...] = jnp.concatenate(near, axis=0).astype(bf16)
    reach = tile_rows + 2
    side = 2 - 2 * col_odd
    total = jnp.zeros((outer.shape[0], far[0].shape[1]), f32)
    spare = [jnp.zeros_like(far[0])] * (outer.shape[0] - tile_rows)
    for f in range(3):
        rows = far[f * reach : (f + 1) * reach]
        if f == 2:
            live = activate(jnp.concatenate(rows, axis=0), line(gain_one))
            rows = [live[r : r + 1] for r in range(reach)]
        for a in range(3):
            taken = jnp.concatenate(rows[a : a + tile_rows] + spare, axis=0).astype(bf16)
            total += jnp.dot(taken, weight[f, a, side], preferred_element_type=f32)
    outer[...] = total


def conv_kernel(
    tile_rows,
    tile_cols,
    channels,
    cache,
    hidden,
    row_a,
    row_b,
    inner,
    gain_one,
    weight,
    convolved,
    stack,
):
    row_even = lax.rem(lax.axis_index("rows"), 2) == 0
    col_even = lax.rem(lax.axis_index("cols"), 2) == 0
    place = lax.broadcasted_iota(jnp.int32, (tile_cols, channels), 0)
    reach = tile_rows + 2
    beside = inner[...].astype(f32)
    gain = line(gain_one)
    for f in range(3):
        side_rows = beside[f * reach : (f + 1) * reach]
        if f == 2:
            side_rows = activate(side_rows, gain)
        left_rows = jnp.where(col_even, 0.0, side_rows)
        right_rows = jnp.where(col_even, side_rows, 0.0)
        for r in range(reach):
            if r == 0 or r == reach - 1:
                one, two = row_a[f].astype(f32), row_b[f].astype(f32)
                row = jnp.where(row_even, two, one) if r == 0 else jnp.where(row_even, one, two)
            elif f < 2:
                row = cache[0, f, r - 1].astype(f32)
            else:
                row = hidden[0, r - 1].astype(f32)
            if f == 2:
                row = activate(row, gain)
            from_left = jnp.where(place == 0, left_rows[r : r + 1], pltpu.roll(row, 1, 0))
            from_right = jnp.where(
                place == tile_cols - 1, right_rows[r : r + 1], pltpu.roll(row, tile_cols - 1, 0)
            )
            rows = pl.ds(r * tile_cols, tile_cols)
            stack[f, rows, 0:channels] = from_left.astype(bf16)
            stack[f, rows, channels : 2 * channels] = row.astype(bf16)
            stack[f, rows, 2 * channels : 3 * channels] = from_right.astype(bf16)
    total = jnp.zeros((tile_rows * tile_cols, channels), f32)
    for f in range(3):
        for a in range(3):
            total += jnp.dot(
                stack[f, a * tile_cols : (a + tile_rows) * tile_cols, :],
                weight[f, a].reshape(3 * channels, channels),
                preferred_element_type=f32,
            )
    convolved[...] = total


def mix_kernel(
    tile_rows, tile_cols, convolved, outer, shortcut, conv_bias, gain_two, normed, mixed
):
    col_even = lax.rem(lax.axis_index("cols"), 2) == 0
    channels = shortcut.shape[-1]
    edge = jnp.where(col_even, 0, tile_cols - 1)
    place = lax.broadcasted_iota(jnp.int32, (tile_cols, channels), 0)
    bias, gain = line(conv_bias), line(gain_two)
    for r in range(tile_rows):
        rows = pl.ds(r * tile_cols, tile_cols)
        total = convolved[rows, :] + jnp.where(place == edge, outer[r : r + 1, :], 0.0)
        kept = (shortcut[0, r].astype(f32) + (total + bias)).astype(bf16)
        mixed[rows, :] = kept
        normed[rows, :] = normalize(kept.astype(f32), gain).astype(bf16)


def query_kernel(score_scale, parts, *refs):
    sources = refs[:parts]
    query_weight, query_bias, key_weight, out = refs[parts:]
    at = 0
    for source in sources:
        rows = source.shape[0]
        queries = (
            jnp.dot(source[...], query_weight[...], preferred_element_type=f32) + line(query_bias)
        ).astype(bf16)
        turned = lax.dot_general(
            queries, key_weight[...], (((1,), (1,)), ((), ())), preferred_element_type=f32
        )
        out[at : at + rows] = (turned * score_scale).astype(bf16)
        at += rows


def pack(out, values, log_sum):
    count, channels = values.shape
    lane = lax.broadcasted_iota(jnp.int32, (count, stat_lanes), 1)
    high = log_sum.astype(bf16).astype(f32)
    rest = log_sum - high
    middle = rest.astype(bf16).astype(f32)
    low = rest - middle
    stats = jnp.where(
        lane == 0, high, jnp.where(lane == 1, middle, jnp.where(lane == 2, low, 0.0))
    )
    out[0:count, :] = values.astype(bf16)
    flat = jnp.transpose(stats)[0:stat_rows, :]
    fill = jnp.zeros((stat_rows, channels - count), f32)
    out[count : count + stat_rows, :] = jnp.concatenate([flat, fill], axis=1).astype(bf16)


def weigh(own, keys, state=None):
    scores = [
        lax.dot_general(own, key[...], (((1,), (1,)), ((), ())), preferred_element_type=f32)
        for key in keys
    ]
    tops = [jnp.max(s, axis=1, keepdims=True) for s in scores]
    top = functools.reduce(jnp.maximum, tops if state is None else tops + [state[0]])
    expos = [jnp.exp(s - top) for s in scores]
    total = sum(jnp.sum(e, axis=1, keepdims=True) for e in expos)
    weighted = sum(
        jnp.dot(e.astype(bf16), key[...], preferred_element_type=f32)
        for e, key in zip(expos, keys)
    )
    if state is not None:
        scale = jnp.exp(state[0] - top)
        total += state[1] * scale
        weighted += state[2] * scale
    return top, total, weighted


def early_kernel(tile, blocks, *refs):
    queries, keys = refs[0], refs[1 : 1 + blocks]
    tops, totals, weights = refs[1 + blocks :]
    for at in range(0, queries.shape[0], tile):
        rows = pl.ds(at, tile)
        top, total, weighted = weigh(queries[rows, :], keys)
        tops[rows, :] = jnp.broadcast_to(top, (tile, stat_lanes))
        totals[rows, :] = jnp.broadcast_to(total, (tile, stat_lanes))
        weights[rows, :] = weighted


def fold_kernel(value_weight, value_bias, out_weight, out_bias, weight, bias):
    weight[...] = jnp.dot(
        value_weight[...], out_weight[...], preferred_element_type=f32
    ).astype(bf16)
    shift = jnp.broadcast_to(line(value_bias), bias.shape)
    high = shift.astype(bf16)
    low = (shift - high.astype(f32)).astype(bf16)
    moved = sum(jnp.dot(v, out_weight[...], preferred_element_type=f32) for v in (high, low))
    bias[...] = moved + line(out_bias)


def late_kernel(tile, blocks, first, *refs):
    queries, tops, totals, weights = refs[:4]
    keys, outs = refs[4 : 4 + blocks], list(refs[4 + blocks :])
    block = first
    while outs:
        rows = pl.ds(block * tile, tile)
        state = (tops[rows, 0:1], totals[rows, 0:1], weights[rows, :])
        top, total, weighted = weigh(queries[rows, :], keys, state)
        mean, log_sum = weighted / total, top + jnp.log(total)
        if block == 0:
            weight, own, own_log = outs.pop(0), outs.pop(0), outs.pop(0)
            own[...] = jnp.dot(mean.astype(bf16), weight[...], preferred_element_type=f32)
            own_log[...] = jnp.broadcast_to(log_sum, (tile, stat_lanes))
        else:
            pack(outs.pop(0), mean, log_sum)
        block += 1


def unpack(ref, count):
    flat = ref[count : count + stat_rows, 0:count].astype(f32)
    stats = jnp.transpose(jnp.concatenate([flat] * (stat_lanes // stat_rows), axis=0))
    return ref[0:count, :].astype(f32), jnp.sum(stats[:, 0:3], axis=1, keepdims=True)


def merge(parts):
    top = functools.reduce(jnp.maximum, [log_sum for _, log_sum in parts])
    scales = [jnp.exp(log_sum - top) for _, log_sum in parts]
    total = sum(scales)
    mean = sum(values * scale for (values, _), scale in zip(parts, scales)) / total
    return mean, top + jnp.log(total)


def final_kernel(tile, others, *refs):
    own, own_log = refs[:2]
    received = refs[2 : 2 + others]
    mixed, weight, bias, decoded = refs[2 + others :]
    parts = [(own[...], own_log[:, 0:1])]
    for ref in received:
        values, log_sum = unpack(ref, tile)
        projected = jnp.dot(values.astype(bf16), weight[...], preferred_element_type=f32)
        parts.append((projected, log_sum))
    mean, _ = merge(parts)
    decoded[...] = (mixed[...].astype(f32) + (mean + bias[0:1, :])).astype(bf16)


def call(kernel, out_shape, *operands, scratch_shapes=()):
    return pl.pallas_call(
        kernel,
        out_shape=out_shape,
        in_specs=[VMEM] * len(operands),
        out_specs=jax.tree.map(lambda _: VMEM, out_shape),
        scratch_shapes=scratch_shapes,
        compiler_params=pltpu.CompilerParams(vmem_limit_bytes=small_grant),
    )(*[pltpu.with_memory_space_constraint(operand, pltpu.VMEM) for operand in operands])


def per_device(
    hidden,
    frame_cache,
    shortcut,
    gain_one,
    conv_weight,
    conv_bias,
    gain_two,
    query_weight,
    query_bias,
    key_weight,
    value_weight,
    value_bias,
    out_weight,
    out_bias,
):
    _, tile_rows, tile_cols, channels = hidden.shape
    tile = tile_rows * tile_cols
    row_count, col_count = lax.axis_size("rows"), lax.axis_size("cols")
    chip_count = col_count // 2
    wide = pltpu.VMEM((tile, channels), bf16)

    edge_rows = pltpu.VMEM((3, tile_cols, channels), bf16)
    row_a, row_b = pl.pallas_call(
        functools.partial(rows_kernel, tile_rows),
        out_shape=(edge_rows, edge_rows),
        in_specs=[ANY, ANY],
        out_specs=(VMEM, VMEM),
        scratch_shapes=[pltpu.SemaphoreType.DMA((6,))],
        compiler_params=pltpu.CompilerParams(vmem_limit_bytes=small_grant),
        cost_estimate=stage_cost,
        name="edge_rows",
    )(*[pltpu.with_memory_space_constraint(v, pltpu.HBM) for v in (frame_cache, hidden)])
    row_a = lax.ppermute(row_a, "rows", near_pairs(row_count, 0))
    row_b = lax.ppermute(row_b, "rows", near_pairs(row_count, 1))
    inner, outer = call(
        functools.partial(cols_kernel, tile_rows, tile_cols),
        (
            pltpu.VMEM((3 * (tile_rows + 2), channels), bf16),
            pltpu.VMEM((-(-tile_rows // 8) * 8, channels), f32),
        ),
        frame_cache,
        hidden,
        row_a,
        row_b,
        gain_one,
        conv_weight,
    )
    inner = lax.ppermute(inner, "cols", near_pairs(col_count, 0))
    outer = lax.ppermute(outer, "cols", near_pairs(col_count, 1))
    convolved = call(
        functools.partial(conv_kernel, tile_rows, tile_cols, channels),
        pltpu.VMEM((tile, channels), f32),
        frame_cache,
        hidden,
        row_a,
        row_b,
        inner,
        gain_one,
        conv_weight,
        scratch_shapes=[
            pltpu.VMEM((3, (tile_rows + 2) * tile_cols, 3 * channels), bf16),
        ],
    )
    normed, mixed = call(
        functools.partial(mix_kernel, tile_rows, tile_cols),
        (wide, wide),
        convolved,
        outer,
        shortcut,
        conv_bias,
        gain_two,
    )

    weight, bias = call(
        fold_kernel,
        (pltpu.VMEM((channels, channels), bf16), pltpu.VMEM((8, channels), f32)),
        value_weight,
        value_bias,
        out_weight,
        out_bias,
    )

    partners = near_pairs(col_count, 0)
    arrived = {0: normed}
    for step in range(row_count - 1, 0, -1):
        arrived[step] = lax.ppermute(normed, "rows", far_pairs(row_count, step))
    query_blocks = [normed]
    for step in range(1, chip_count):
        query_blocks.append(lax.ppermute(normed, "cols", far_pairs(chip_count, step, 2)))
    keys = {}
    for step, block in arrived.items():
        keys[step] = [block, lax.ppermute(block, "cols", partners)]
    early = keys[0]
    late = [key for step in range(row_count - 1, 0, -1) for key in keys[step]]

    query_rows = chip_count * tile
    queries = call(
        functools.partial(query_kernel, float(channels) ** (-0.5), chip_count),
        pltpu.VMEM((query_rows, channels), bf16),
        *query_blocks,
        query_weight,
        query_bias,
        key_weight,
    )
    stat = pltpu.VMEM((query_rows, stat_lanes), f32)
    state = call(
        functools.partial(early_kernel, tile, len(early)),
        (stat, stat, pltpu.VMEM((query_rows, channels), f32)),
        queries,
        *early,
    )
    packed = pltpu.VMEM((tile + stat_rows, channels), bf16)
    results = call(
        functools.partial(late_kernel, tile, len(late), 1),
        (packed,) * (chip_count - 1),
        queries,
        *state,
        *late,
    )
    returned = []
    for step, result in enumerate(results, 1):
        returned.append(
            lax.ppermute(result, "cols", [(j, i) for i, j in far_pairs(chip_count, step, 2)])
        )
    own, own_log = call(
        functools.partial(late_kernel, tile, len(late), 0),
        (pltpu.VMEM((tile, channels), f32), pltpu.VMEM((tile, stat_lanes), f32)),
        queries,
        *state,
        *late,
        weight,
    )
    decoded = call(
        functools.partial(final_kernel, tile, chip_count - 1),
        jax.ShapeDtypeStruct((tile, channels), bf16),
        own,
        own_log,
        *returned,
        mixed,
        weight,
        bias,
    )
    return decoded.reshape(1, tile_rows, tile_cols, channels)


def solution(mesh):
    placed = (
        P("videos", "rows", "cols", None),
        P("videos", None, "rows", "cols", None),
        P("videos", "rows", "cols", None),
        P(),
        P(),
        P(),
        P(),
        P(),
        P(),
        P(),
        P(),
        P(),
        P(),
        P(),
    )
    return jax.shard_map(
        per_device,
        mesh=mesh,
        in_specs=placed,
        out_specs=P("videos", "rows", "cols", None),
        check_vma=False,
    )
```

```python
import functools

import jax
import jax.numpy as jnp
from jax import lax
from jax.experimental import pallas as pl
from jax.experimental.pallas import tpu as pltpu
from jax.sharding import PartitionSpec as P


norm_epsilon = 1e-06
stat_lanes = 128
stat_rows = 8
f32 = jnp.float32
bf16 = jnp.bfloat16

small_grant = 24 * 1024 * 1024
stage_cost = pl.CostEstimate(flops=10**10, bytes_accessed=10**7, transcendentals=0)
VMEM = pl.BlockSpec(memory_space=pltpu.VMEM)
SMEM = pl.BlockSpec(memory_space=pltpu.SMEM)
ANY = pl.BlockSpec(memory_space=pl.ANY)


def near_pairs(count, first):
    pairs = []
    for i in range(first, count - 1, 2):
        pairs += [(i, i + 1), (i + 1, i)]
    return pairs


def far_pairs(count, step, stride=1):
    xor = count & (count - 1) == 0
    pairs = []
    for i in range(count):
        j = i ^ step if xor else (i + step) % count
        pairs += [(i * stride + k, j * stride + k) for k in range(stride)]
    return pairs


def normalize(cells, gain):
    mean_square = jnp.mean(cells * cells, axis=-1, keepdims=True)
    return cells * lax.rsqrt(mean_square + norm_epsilon) * gain


def line(ref):
    return ref[...].reshape(1, ref.shape[0])


def activate(cells, gain):
    scaled = normalize(cells, gain)
    return scaled * (1.0 / (1.0 + jnp.exp(-scaled)))


def rows_kernel(tile_rows, cache, hidden, row_a, row_b, sems):
    odd = lax.rem(lax.axis_index("rows"), 2)
    copies = []
    for out, at in ((row_a, (1 - odd) * (tile_rows - 1)), (row_b, odd * (tile_rows - 1))):
        for f in range(3):
            source = cache.at[0, f, at] if f < 2 else hidden.at[0, at]
            copies.append(pltpu.make_async_copy(source, out.at[f], sems.at[len(copies)]))
    for copy in copies:
        copy.start()
    for copy in copies:
        copy.wait()


def cols_kernel(
    tile_rows, tile_cols, cache, hidden, row_a, row_b, gain_one, weight, inner, outer
):
    row_even = lax.rem(lax.axis_index("rows"), 2) == 0
    col_odd = lax.rem(lax.axis_index("cols"), 2)
    col_even = col_odd == 0
    first, last = pl.ds(0, 1), pl.ds(tile_cols - 1, 1)
    near, far = [], []

    def add(pick):
        left, right = pick(first).astype(f32), pick(last).astype(f32)
        near.append(jnp.where(col_even, right, left))
        far.append(jnp.where(col_even, left, right))

    for f in range(3):
        add(lambda at: jnp.where(row_even, row_b[f, at].astype(f32), row_a[f, at].astype(f32)))
        for r in range(tile_rows):
            add(lambda at: cache[0, f, r, at] if f < 2 else hidden[0, r, at])
        add(lambda at: jnp.where(row_even, row_a[f, at].astype(f32), row_b[f, at].astype(f32)))
    inner[...] = jnp.concatenate(near, axis=0).astype(bf16)
    reach = tile_rows + 2
    side = 2 - 2 * col_odd
    total = jnp.zeros((outer.shape[0], far[0].shape[1]), f32)
    spare = [jnp.zeros_like(far[0])] * (outer.shape[0] - tile_rows)
    for f in range(3):
        rows = far[f * reach : (f + 1) * reach]
        if f == 2:
            live = activate(jnp.concatenate(rows, axis=0), line(gain_one))
            rows = [live[r : r + 1] for r in range(reach)]
        for a in range(3):
            taken = jnp.concatenate(rows[a : a + tile_rows] + spare, axis=0).astype(bf16)
            total += jnp.dot(taken, weight[f, a, side], preferred_element_type=f32)
    outer[...] = total


def conv_kernel(
    tile_rows,
    tile_cols,
    channels,
    cache,
    hidden,
    row_a,
    row_b,
    inner,
    gain_one,
    weight,
    convolved,
    stack,
):
    row_even = lax.rem(lax.axis_index("rows"), 2) == 0
    col_even = lax.rem(lax.axis_index("cols"), 2) == 0
    place = lax.broadcasted_iota(jnp.int32, (tile_cols, channels), 0)
    reach = tile_rows + 2
    beside = inner[...].astype(f32)
    gain = line(gain_one)
    for f in range(3):
        side_rows = beside[f * reach : (f + 1) * reach]
        if f == 2:
            side_rows = activate(side_rows, gain)
        left_rows = jnp.where(col_even, 0.0, side_rows)
        right_rows = jnp.where(col_even, side_rows, 0.0)
        for r in range(reach):
            if r == 0 or r == reach - 1:
                one, two = row_a[f].astype(f32), row_b[f].astype(f32)
                row = jnp.where(row_even, two, one) if r == 0 else jnp.where(row_even, one, two)
            elif f < 2:
                row = cache[0, f, r - 1].astype(f32)
            else:
                row = hidden[0, r - 1].astype(f32)
            if f == 2:
                row = activate(row, gain)
            from_left = jnp.where(place == 0, left_rows[r : r + 1], pltpu.roll(row, 1, 0))
            from_right = jnp.where(
                place == tile_cols - 1, right_rows[r : r + 1], pltpu.roll(row, tile_cols - 1, 0)
            )
            rows = pl.ds(r * tile_cols, tile_cols)
            stack[f, rows, 0:channels] = from_left.astype(bf16)
            stack[f, rows, channels : 2 * channels] = row.astype(bf16)
            stack[f, rows, 2 * channels : 3 * channels] = from_right.astype(bf16)
    total = jnp.zeros((tile_rows * tile_cols, channels), f32)
    for f in range(3):
        for a in range(3):
            total += jnp.dot(
                stack[f, a * tile_cols : (a + tile_rows) * tile_cols, :],
                weight[f, a].reshape(3 * channels, channels),
                preferred_element_type=f32,
            )
    convolved[...] = total


def mix_kernel(
    tile_rows, tile_cols, convolved, outer, shortcut, conv_bias, gain_two, normed, mixed
):
    col_even = lax.rem(lax.axis_index("cols"), 2) == 0
    channels = shortcut.shape[-1]
    edge = jnp.where(col_even, 0, tile_cols - 1)
    place = lax.broadcasted_iota(jnp.int32, (tile_cols, channels), 0)
    bias, gain = line(conv_bias), line(gain_two)
    for r in range(tile_rows):
        rows = pl.ds(r * tile_cols, tile_cols)
        total = convolved[rows, :] + jnp.where(place == edge, outer[r : r + 1, :], 0.0)
        kept = (shortcut[0, r].astype(f32) + (total + bias)).astype(bf16)
        mixed[rows, :] = kept
        normed[rows, :] = normalize(kept.astype(f32), gain).astype(bf16)


def query_kernel(score_scale, parts, *refs):
    sources = refs[:parts]
    query_weight, query_bias, key_weight, out = refs[parts:]
    at = 0
    for source in sources:
        rows = source.shape[0]
        queries = (
            jnp.dot(source[...], query_weight[...], preferred_element_type=f32) + line(query_bias)
        ).astype(bf16)
        turned = lax.dot_general(
            queries, key_weight[...], (((1,), (1,)), ((), ())), preferred_element_type=f32
        )
        out[at : at + rows] = (turned * score_scale).astype(bf16)
        at += rows


def pack(out, values, log_sum):
    count, channels = values.shape
    lane = lax.broadcasted_iota(jnp.int32, (count, stat_lanes), 1)
    high = log_sum.astype(bf16).astype(f32)
    rest = log_sum - high
    middle = rest.astype(bf16).astype(f32)
    low = rest - middle
    stats = jnp.where(
        lane == 0, high, jnp.where(lane == 1, middle, jnp.where(lane == 2, low, 0.0))
    )
    out[0:count, :] = values.astype(bf16)
    flat = jnp.transpose(stats)[0:stat_rows, :]
    fill = jnp.zeros((stat_rows, channels - count), f32)
    out[count : count + stat_rows, :] = jnp.concatenate([flat, fill], axis=1).astype(bf16)


def weigh(own, keys, state=None):
    scores = [
        lax.dot_general(own, key[...], (((1,), (1,)), ((), ())), preferred_element_type=f32)
        for key in keys
    ]
    tops = [jnp.max(s, axis=1, keepdims=True) for s in scores]
    top = functools.reduce(jnp.maximum, tops if state is None else tops + [state[0]])
    expos = [jnp.exp(s - top) for s in scores]
    total = sum(jnp.sum(e, axis=1, keepdims=True) for e in expos)
    weighted = sum(
        jnp.dot(e.astype(bf16), key[...], preferred_element_type=f32)
        for e, key in zip(expos, keys)
    )
    if state is not None:
        scale = jnp.exp(state[0] - top)
        total += state[1] * scale
        weighted += state[2] * scale
    return top, total, weighted


def early_kernel(tile, blocks, *refs):
    queries, keys = refs[0], refs[1 : 1 + blocks]
    tops, totals, weights = refs[1 + blocks :]
    for at in range(0, queries.shape[0], tile):
        rows = pl.ds(at, tile)
        top, total, weighted = weigh(queries[rows, :], keys)
        tops[rows, :] = jnp.broadcast_to(top, (tile, stat_lanes))
        totals[rows, :] = jnp.broadcast_to(total, (tile, stat_lanes))
        weights[rows, :] = weighted


def fold_kernel(value_weight, value_bias, out_weight, out_bias, weight, bias):
    weight[...] = jnp.dot(
        value_weight[...], out_weight[...], preferred_element_type=f32
    ).astype(bf16)
    shift = jnp.broadcast_to(line(value_bias), bias.shape)
    high = shift.astype(bf16)
    low = (shift - high.astype(f32)).astype(bf16)
    moved = sum(jnp.dot(v, out_weight[...], preferred_element_type=f32) for v in (high, low))
    bias[...] = moved + line(out_bias)


def middle_kernel(tile, blocks, *refs):
    queries, tops, totals, weights = refs[:4]
    keys, outs = refs[4 : 4 + blocks], refs[4 + blocks :]
    for at in range(0, queries.shape[0], tile):
        rows = pl.ds(at, tile)
        state = (tops[rows, 0:1], totals[rows, 0:1], weights[rows, :])
        top, total, weighted = weigh(queries[rows, :], keys, state)
        outs[0][rows, :] = jnp.broadcast_to(top, (tile, stat_lanes))
        outs[1][rows, :] = jnp.broadcast_to(total, (tile, stat_lanes))
        outs[2][rows, :] = weighted


def late_kernel(tile, blocks, first, *refs):
    queries, tops, totals, weights = refs[:4]
    keys, outs = refs[4 : 4 + blocks], list(refs[4 + blocks :])
    block = first
    while outs:
        rows = pl.ds(block * tile, tile)
        state = (tops[rows, 0:1], totals[rows, 0:1], weights[rows, :])
        top, total, weighted = weigh(queries[rows, :], keys, state)
        mean, log_sum = weighted / total, top + jnp.log(total)
        if block == 0:
            weight, own, own_log = outs.pop(0), outs.pop(0), outs.pop(0)
            own[...] = jnp.dot(mean.astype(bf16), weight[...], preferred_element_type=f32)
            own_log[...] = jnp.broadcast_to(log_sum, (tile, stat_lanes))
        else:
            pack(outs.pop(0), mean, log_sum)
        block += 1


def unpack(ref, count):
    flat = ref[count : count + stat_rows, 0:count].astype(f32)
    stats = jnp.transpose(jnp.concatenate([flat] * (stat_lanes // stat_rows), axis=0))
    return ref[0:count, :].astype(f32), jnp.sum(stats[:, 0:3], axis=1, keepdims=True)


def merge(parts):
    top = functools.reduce(jnp.maximum, [log_sum for _, log_sum in parts])
    scales = [jnp.exp(log_sum - top) for _, log_sum in parts]
    total = sum(scales)
    mean = sum(values * scale for (values, _), scale in zip(parts, scales)) / total
    return mean, top + jnp.log(total)


def final_kernel(tile, others, *refs):
    own, own_log = refs[:2]
    received = refs[2 : 2 + others]
    mixed, weight, bias, decoded = refs[2 + others :]
    parts = [(own[...], own_log[:, 0:1])]
    for ref in received:
        values, log_sum = unpack(ref, tile)
        projected = jnp.dot(values.astype(bf16), weight[...], preferred_element_type=f32)
        parts.append((projected, log_sum))
    mean, _ = merge(parts)
    decoded[...] = (mixed[...].astype(f32) + (mean + bias[0:1, :])).astype(bf16)


def call(kernel, out_shape, *operands, scratch_shapes=()):
    return pl.pallas_call(
        kernel,
        out_shape=out_shape,
        in_specs=[VMEM] * len(operands),
        out_specs=jax.tree.map(lambda _: VMEM, out_shape),
        scratch_shapes=scratch_shapes,
        compiler_params=pltpu.CompilerParams(vmem_limit_bytes=small_grant),
    )(*[pltpu.with_memory_space_constraint(operand, pltpu.VMEM) for operand in operands])


def per_device(
    hidden,
    frame_cache,
    shortcut,
    gain_one,
    conv_weight,
    conv_bias,
    gain_two,
    query_weight,
    query_bias,
    key_weight,
    value_weight,
    value_bias,
    out_weight,
    out_bias,
):
    _, tile_rows, tile_cols, channels = hidden.shape
    tile = tile_rows * tile_cols
    row_count, col_count = lax.axis_size("rows"), lax.axis_size("cols")
    chip_count = col_count // 2
    wide = pltpu.VMEM((tile, channels), bf16)

    edge_rows = pltpu.VMEM((3, tile_cols, channels), bf16)
    row_a, row_b = pl.pallas_call(
        functools.partial(rows_kernel, tile_rows),
        out_shape=(edge_rows, edge_rows),
        in_specs=[ANY, ANY],
        out_specs=(VMEM, VMEM),
        scratch_shapes=[pltpu.SemaphoreType.DMA((6,))],
        compiler_params=pltpu.CompilerParams(vmem_limit_bytes=small_grant),
        cost_estimate=stage_cost,
        name="edge_rows",
    )(*[pltpu.with_memory_space_constraint(v, pltpu.HBM) for v in (frame_cache, hidden)])
    row_a = lax.ppermute(row_a, "rows", near_pairs(row_count, 0))
    row_b = lax.ppermute(row_b, "rows", near_pairs(row_count, 1))
    inner, outer = call(
        functools.partial(cols_kernel, tile_rows, tile_cols),
        (
            pltpu.VMEM((3 * (tile_rows + 2), channels), bf16),
            pltpu.VMEM((-(-tile_rows // 8) * 8, channels), f32),
        ),
        frame_cache,
        hidden,
        row_a,
        row_b,
        gain_one,
        conv_weight,
    )
    inner = lax.ppermute(inner, "cols", near_pairs(col_count, 0))
    outer = lax.ppermute(outer, "cols", near_pairs(col_count, 1))
    convolved = call(
        functools.partial(conv_kernel, tile_rows, tile_cols, channels),
        pltpu.VMEM((tile, channels), f32),
        frame_cache,
        hidden,
        row_a,
        row_b,
        inner,
        gain_one,
        conv_weight,
        scratch_shapes=[
            pltpu.VMEM((3, (tile_rows + 2) * tile_cols, 3 * channels), bf16),
        ],
    )
    normed, mixed = call(
        functools.partial(mix_kernel, tile_rows, tile_cols),
        (wide, wide),
        convolved,
        outer,
        shortcut,
        conv_bias,
        gain_two,
    )

    weight, bias = call(
        fold_kernel,
        (pltpu.VMEM((channels, channels), bf16), pltpu.VMEM((8, channels), f32)),
        value_weight,
        value_bias,
        out_weight,
        out_bias,
    )

    partners = near_pairs(col_count, 0)
    arrived = {0: normed}
    for step in range(row_count - 1, 0, -1):
        arrived[step] = lax.ppermute(normed, "rows", far_pairs(row_count, step))
    query_blocks = [normed]
    for step in range(1, chip_count):
        query_blocks.append(lax.ppermute(normed, "cols", far_pairs(chip_count, step, 2)))
    keys = {}
    for step, block in arrived.items():
        keys[step] = [block, lax.ppermute(block, "cols", partners)]
    early = keys[0]
    middle = keys[row_count - 1]
    late = [key for step in range(row_count - 2, 0, -1) for key in keys[step]]

    query_rows = chip_count * tile
    queries = call(
        functools.partial(query_kernel, float(channels) ** (-0.5), chip_count),
        pltpu.VMEM((query_rows, channels), bf16),
        *query_blocks,
        query_weight,
        query_bias,
        key_weight,
    )
    stat = pltpu.VMEM((query_rows, stat_lanes), f32)
    state = call(
        functools.partial(early_kernel, tile, len(early)),
        (stat, stat, pltpu.VMEM((query_rows, channels), f32)),
        queries,
        *early,
    )
    state = call(
        functools.partial(middle_kernel, tile, len(middle)),
        (stat, stat, pltpu.VMEM((query_rows, channels), f32)),
        queries,
        *state,
        *middle,
    )
    packed = pltpu.VMEM((tile + stat_rows, channels), bf16)
    results = call(
        functools.partial(late_kernel, tile, len(late), 1),
        (packed,) * (chip_count - 1),
        queries,
        *state,
        *late,
    )
    returned = []
    for step, result in enumerate(results, 1):
        returned.append(
            lax.ppermute(result, "cols", [(j, i) for i, j in far_pairs(chip_count, step, 2)])
        )
    own, own_log = call(
        functools.partial(late_kernel, tile, len(late), 0),
        (pltpu.VMEM((tile, channels), f32), pltpu.VMEM((tile, stat_lanes), f32)),
        queries,
        *state,
        *late,
        weight,
    )
    decoded = call(
        functools.partial(final_kernel, tile, chip_count - 1),
        jax.ShapeDtypeStruct((tile, channels), bf16),
        own,
        own_log,
        *returned,
        mixed,
        weight,
        bias,
    )
    return decoded.reshape(1, tile_rows, tile_cols, channels)


def solution(mesh):
    placed = (
        P("videos", "rows", "cols", None),
        P("videos", None, "rows", "cols", None),
        P("videos", "rows", "cols", None),
        P(),
        P(),
        P(),
        P(),
        P(),
        P(),
        P(),
        P(),
        P(),
        P(),
        P(),
    )
    return jax.shard_map(
        per_device,
        mesh=mesh,
        in_specs=placed,
        out_specs=P("videos", "rows", "cols", None),
        check_vma=False,
    )
```
